512 devices in a mesh: lat: 64 (over z, x, core), rad: 8 (over y).
Axes of the slice: x: 4, y: 8, z: 8, core: 2. Of those that a mesh axis runs over, the one named last changes fastest.
Arguments:
- fourier: bfloat16 [2, 2, 256, 2, 64, 1152], P(None, None, 'rad', None, None, 'lat'), may hold values from -6 to 6
- legendre: bfloat16 [64, 1024, 1152], P('lat'), may hold values from -0.1875 to 0.1875
- inverse: bfloat16 [1024, 512, 512], P('lat', 'rad'), may hold values from -0.25 to 0.25
- order_of_slot: int32 [64], replicated, may hold values from 0 to 63, each once
- degree_of_slot: int32 [1024], replicated, may hold values from 0 to 1023, each once
- degree_count: int32 [64], replicated, may hold values from 1 to 1024, as said below
Outputs:
- solved: float32 [1024, 512, 2, 64], P('lat', 'rad')
The draws below stay inside these ranges and needn't reach their ends.
Inputs may be any that keep to these rules, and one draw needn't show every extreme that they name: `order_of_slot`: a permutation; the index p of lat is given slot p. `degree_of_slot`: a permutation; the index p of lat is given slots p * 16 to (p + 1) * 16 - 1. Order k is live on the last degree_count[k] degrees of the band; some order has all 1024.
All inputs are finite; a program needn't handle non-finite values.
Results may differ from the reference program's by a relative error of at most 0.0042.
Values may be sent and summed in bfloat16 or wider, within the bound.
A program may use at most 64 MiB of HBM per device.

```python
import jax
import jax.numpy as jnp
from jax import lax

NH = 1152
NR = 256
M = 64
NDEG = 1024


def draw_degree_count(key, part):
    drawn = jax.random.randint(key, (M,), 1, NDEG + 1)
    longest = jax.random.randint(jax.random.fold_in(key, 7), (), 0, M)
    return jnp.where(jnp.arange(M) == longest, NDEG, drawn).astype(jnp.int32)


def level_of(own_key, dims, split, least, largest):
    level = 1.0
    for dim, shards_of in split:
        draws = jax.random.uniform(jax.random.fold_in(jax.random.fold_in(own_key, 6), dim), (shards_of,), jnp.float32, least / len(split), largest / len(split))
        level = level * jnp.repeat(jnp.exp(draws), dims[dim] // shards_of).reshape((-1,) + (1,) * (len(dims) - 1 - dim))
    return level


def bell_draw(own_key, dims, width, limit, shards=(), kind=jnp.bfloat16):
    values = jax.random.normal(own_key, dims, jnp.float32) * width
    if len(shards) > 0:
        values = level_of(own_key, dims, shards, -0.22, 0.18) * values
    return jnp.clip(values, min=-limit, max=limit).astype(kind)


def setup_inputs(seed: int = 0) -> dict:
    key_list = jax.random.split(jax.random.key(seed), 7)
    return {
        "fourier": bell_draw(key_list[0], (2, 2, NR, 2, M, NH), 1.0, 6.0, ((2, 8), (5, 64))),
        "legendre": bell_draw(key_list[1], (M, NDEG, NH), NH ** -0.5, 0.1875, ((0, 64),)),
        "inverse": bell_draw(key_list[2], (NDEG, 2 * NR, 2 * NR), (2 * NR) ** -0.5, 0.25, ((0, 64), (1, 8))),
        "order_of_slot": jax.random.permutation(key_list[3], M).astype(jnp.int32),
        "degree_of_slot": jax.random.permutation(key_list[4], NDEG).astype(jnp.int32),
        "degree_count": draw_degree_count(jax.random.fold_in(key_list[6], 71), 0),
    }


def reference(fourier, legendre, inverse, order_of_slot, degree_of_slot, degree_count):
    picked = jnp.take(fourier, order_of_slot.astype(jnp.int32), axis=4)
    north_rows = picked[:, :, :, 0].astype(jnp.float32)
    south_rows = picked[:, :, :, 1].astype(jnp.float32)
    even_part = (north_rows + south_rows).astype(jnp.bfloat16)
    odd_part = (north_rows - south_rows).astype(jnp.bfloat16)
    counts = jnp.take(degree_count, order_of_slot.astype(jnp.int32))
    first_live = (NDEG - counts).astype(jnp.int32)
    band_index = jnp.arange(NDEG, dtype=jnp.int32)
    live_mask = band_index[None, :] >= first_live[:, None]
    use_even = ((band_index[None, :] - first_live[:, None]) % 2) == 0

    def one_slot(inputs):
        table, even_slot, odd_slot, live_row, even_row = inputs
        from_even = jnp.dot(table, even_slot.reshape(-1, NH).T, preferred_element_type=jnp.float32)
        from_odd = jnp.dot(table, odd_slot.reshape(-1, NH).T, preferred_element_type=jnp.float32)
        chosen = jnp.where(even_row[:, None], from_even, from_odd)
        return jnp.where(live_row[:, None], chosen, jnp.float32(0.0)).astype(jnp.bfloat16)

    coefficients = lax.map(one_slot, (legendre, jnp.moveaxis(even_part, 3, 0), jnp.moveaxis(odd_part, 3, 0), live_mask, use_even))
    regrouped = jnp.take(coefficients, degree_of_slot.astype(jnp.int32), axis=1)
    regrouped = regrouped.reshape(M, NDEG, 2, 2, NR)

    def one_degree(inputs):
        matrix, block_rows = inputs
        right_side = jnp.transpose(block_rows, (1, 3, 2, 0)).reshape(2 * NR, 2 * M)
        product = jnp.dot(matrix, right_side, preferred_element_type=jnp.float32)
        return product.reshape(2 * NR, 2, M)

    return lax.map(one_degree, (inverse, jnp.moveaxis(regrouped, 1, 0)))
```

```python
import functools

import jax
import jax.numpy as jnp
from jax import lax
from jax.experimental import pallas as pl
from jax.experimental.pallas import tpu as pltpu
from jax.sharding import PartitionSpec as P

BF16 = jnp.bfloat16
F32 = jnp.float32
MESH = pl.DeviceIdType.MESH
LANES = 128
CHUNKS = 4


def iota(shape, dim):
    return lax.broadcasted_iota(jnp.int32, shape, dim)


def column(row):
    return jnp.transpose(jnp.broadcast_to(row, (LANES, row.shape[1])))


def dot_nt(a, b):
    return lax.dot_general(a, b, (((1,), (1,)), ((), ())), preferred_element_type=F32)


def kernel(
    dims,
    order_ref, degree_ref, count_ref, rows_hbm, table_hbm, inverse_hbm,
    out_ref,
    rows, table, inverse, north, south, send_even, send_odd, recv_even, recv_odd,
    pick, column_degree, table_live, send_c, recv_c, wide, gathered, spread, total,
    rows_sem, table_sem, inverse_sem, send1, recv1, send2, recv2,
    send_up, send_down, recv_up, recv_down,
):
    n_lat, n_rad, n_l, n_deg, n_t = dims
    me = lax.axis_index("lat")
    y = lax.axis_index("rad")
    up, down = lax.rem(y + 1, n_rad), lax.rem(y + n_rad - 1, n_rad)
    group = min(8, n_lat)
    planes = n_lat // group

    def load_rows(l):
        return pltpu.make_async_copy(rows_hbm.at[:, l], rows.at[l], rows_sem.at[l])

    for l in range(n_l):
        load_rows(l).start()
    load_table = pltpu.make_async_copy(table_hbm, table, table_sem)
    load_table.start()
    load_inverse = pltpu.make_async_copy(inverse_hbm, inverse, inverse_sem)
    load_inverse.start()

    barrier = pltpu.get_barrier_semaphore()

    def greet(k, carry):
        pl.semaphore_signal(
            barrier, inc=1, device_id={"lat": lax.rem(me + k, n_lat)}, device_id_type=MESH
        )
        return carry

    lax.fori_loop(1, n_lat, greet, 0)
    for other in (up, down):
        pl.semaphore_signal(barrier, inc=1, device_id={"rad": other}, device_id_type=MESH)

    order = order_ref[...].astype(F32)
    order_column = column(order)[:, :n_lat]
    order_pick = jnp.where(
        order_column == iota((n_lat, n_lat), 1).astype(F32), 1.0, 0.0
    ).astype(BF16)
    for l in range(n_l):
        load_rows(l).wait()
        picked = dot_nt(order_pick, rows.at[l].reshape(2 * LANES, n_lat)[...])
        north[pl.ds(l, n_lat, stride=n_l), :] = picked[:, :LANES]
        south[pl.ds(l, n_lat, stride=n_l), :] = picked[:, LANES:]

    source, target = iota((2 * LANES, 2 * LANES), 0), iota((2 * LANES, 2 * LANES), 1)
    fold = jnp.where(
        source // 2 == target % LANES,
        jnp.where((source % 2 == 1) & (target >= LANES), -1.0, 1.0),
        0.0,
    ).astype(BF16)

    pl.semaphore_wait(barrier, n_lat + 1)

    def fold_and_send(k, carry):
        far = lax.select(lax.rem(k, 2) == 0, k // 2, lax.rem(planes - k // 2, planes))
        plane = lax.rem(me // group + far, planes)
        at = pl.ds(pl.multiple_of(plane * (group * n_l), 16), group * n_l)
        both = jnp.concatenate([north[at, :], south[at, :]], axis=1).astype(BF16)
        folded = jnp.dot(both, fold, preferred_element_type=F32).astype(BF16)
        send_even.reshape(n_lat * n_l, LANES)[at, :] = folded[:, :LANES]
        send_odd.reshape(n_lat * n_l, LANES)[at, :] = folded[:, LANES:]

        def send(i, c):
            peer = plane * group + lax.rem(me + i, group)

            @pl.when(peer != me)
            def _():
                for p, (src, dst) in enumerate(((send_even, recv_even), (send_odd, recv_odd))):
                    pltpu.make_async_remote_copy(
                        src_ref=src.at[peer], dst_ref=dst.at[me],
                        send_sem=send1.at[p], recv_sem=recv1.at[p],
                        device_id={"lat": peer}, device_id_type=MESH,
                    ).start()

            @pl.when(peer == me)
            def _():
                for p, (src, dst) in enumerate(((send_even, recv_even), (send_odd, recv_odd))):
                    pltpu.make_async_copy(src.at[me], dst.at[me], recv1.at[p]).start()

            return c

        return lax.fori_loop(0, group, send, carry)

    lax.fori_loop(1, planes + 1, fold_and_send, 0)

    mine = jnp.sum(jnp.where(iota((1, n_lat), 1) == me, order, 0.0), axis=1, keepdims=True)
    count = jnp.sum(
        jnp.where(iota((1, n_lat), 1).astype(F32) == mine, count_ref[...].astype(F32), 0.0),
        axis=1, keepdims=True,
    )
    first = n_deg - count
    blocks, block = degree_ref.shape

    def pick_rows(b, carry):
        at = pl.ds(pl.multiple_of(b * block, block), block)
        held = column(degree_ref[pl.ds(b, 1), :].astype(F32))
        column_degree[at, :] = held
        for j in range(blocks):
            lane = (iota((block, block), 1) + j * block).astype(F32)
            cell = held[:, :block]
            pick[at, j * block:(j + 1) * block] = jnp.where(
                (cell == lane) & (cell >= first), 1.0, 0.0
            ).astype(BF16)
        return carry

    lax.fori_loop(0, blocks, pick_rows, 0)
    load_table.wait()
    rows_at_once = min(256, n_deg)

    def order_rows(b, carry):
        at = pl.ds(pl.multiple_of(b * rows_at_once, rows_at_once), rows_at_once)
        table_live[at, :] = jnp.dot(
            pick[at, :], table[...], preferred_element_type=F32
        ).astype(BF16)
        return carry

    lax.fori_loop(0, n_deg // rows_at_once, order_rows, 0)

    pltpu.make_async_copy(recv_even, recv_even, recv1.at[0]).wait()
    pltpu.make_async_copy(recv_odd, recv_odd, recv1.at[1]).wait()

    parts = n_deg // rows_at_once
    slots_at_once = rows_at_once // n_t

    def analyse_and_send(k, carry):
        part = lax.rem(me // slots_at_once + k, parts)
        at = pl.ds(pl.multiple_of(part * rows_at_once, rows_at_once), rows_at_once)
        both = jnp.concatenate(
            [
                recv_even.reshape(n_lat * n_l, LANES)[...],
                recv_odd.reshape(n_lat * n_l, LANES)[...],
            ],
            axis=1,
        )
        product = jnp.dot(table_live[at, :], both, preferred_element_type=F32)
        parity = (column_degree[at, :] - first).astype(jnp.int32) & 1
        send_c[at, :] = jnp.where(
            parity == 0, product[:, :LANES], product[:, LANES:]
        ).astype(BF16)

        def send(i, c):
            peer = part * slots_at_once + lax.rem(me + i, slots_at_once)
            src = send_c.at[pl.ds(pl.multiple_of(peer * n_t, n_t), n_t), :]
            dst = recv_c.at[pl.ds(pl.multiple_of(me * n_t, n_t), n_t), :]

            @pl.when(peer != me)
            def _():
                pltpu.make_async_remote_copy(
                    src_ref=src, dst_ref=dst, send_sem=send2, recv_sem=recv2,
                    device_id={"lat": peer}, device_id_type=MESH,
                ).start()

            @pl.when(peer == me)
            def _():
                pltpu.make_async_copy(src, dst, recv2).start()

            return c

        return lax.fori_loop(0, slots_at_once, send, carry)

    lax.fori_loop(0, parts, analyse_and_send, 0)

    load_inverse.wait()
    flat_inverse = inverse.reshape(inverse.shape[0] * inverse.shape[1], inverse.shape[2])
    n_q, full = inverse.shape[1], inverse.shape[2]
    radii = full // 2 // n_rad

    def spread_columns(o, carry):
        row, col = iota((full, 2 * LANES), 0), iota((full, 2 * LANES), 1)
        lane = col % LANES
        wanted = (lane // (2 * radii)) * (full // 2) + o * radii + lane % radii
        part = (lane // radii) % 2
        place = jnp.where((row == wanted) & (part == col // LANES), 1.0, 0.0).astype(BF16)
        placed = jnp.dot(flat_inverse[...], place, preferred_element_type=F32).astype(BF16)
        for t in range(n_t):
            for c in range(2):
                spread[o, t, c * n_q:(c + 1) * n_q, :] = placed[
                    t * n_q:(t + 1) * n_q, c * LANES:(c + 1) * LANES
                ]
        return carry

    lax.fori_loop(0, n_rad, spread_columns, 0)

    pltpu.make_async_copy(recv_c, recv_c, recv2).wait()
    wide[...] = recv_c[...].astype(F32)
    for t in range(n_t):
        gathered[y, t] = wide[pl.ds(t, n_lat, stride=n_t), :].astype(BF16)

    per = n_t // CHUNKS
    half = n_rad // 2

    def pass_on(upwards, origin, step, c):
        sems = (send_up, recv_up) if upwards else (send_down, recv_down)
        block_ref = gathered.at[origin, pl.ds(c * per, per)]
        return pltpu.make_async_remote_copy(
            src_ref=block_ref, dst_ref=block_ref,
            send_sem=sems[0].at[step], recv_sem=sems[1].at[step, c],
            device_id={"rad": up if upwards else down}, device_id_type=MESH,
        )

    def send_own(c, carry):
        pass_on(True, y, 0, c).start()
        pass_on(False, y, 0, c).start()
        return carry

    lax.fori_loop(0, CHUNKS, send_own, 0)

    def add(origins, c, init):
        for i in range(per):
            t = c * per + i
            a = [spread[o, t] for o in origins]
            b = [gathered[o, t] for o in origins]
            a = a[0] if len(a) == 1 else jnp.concatenate(a, axis=1)
            b = b[0] if len(b) == 1 else jnp.concatenate(b, axis=1)
            term = dot_nt(a, b)
            if init:
                total[t] = term
            else:
                total[t] += term

    def add_own(c, carry):
        add([y], c, True)
        return carry

    lax.fori_loop(0, CHUNKS, add_own, 0)

    for step in range(1, half):
        below, above = lax.rem(y + n_rad - step, n_rad), lax.rem(y + step, n_rad)

        def relay(c, carry):
            pass_on(True, below, step - 1, c).wait_recv()
            if step < half - 1:
                pass_on(True, below, step, c).start()
            else:
                @pl.when(c < CHUNKS // 2)
                def _():
                    pass_on(True, below, step, c).start()
            pass_on(False, above, step - 1, c).wait_recv()
            if step < half - 1:
                pass_on(False, above, step, c).start()
            else:
                @pl.when(c >= CHUNKS // 2)
                def _():
                    pass_on(False, above, step, c).start()
            add([below, above], c, False)
            return carry

        lax.fori_loop(0, CHUNKS, relay, 0)

    opposite = lax.rem(y + half, n_rad)
    for c in range(CHUNKS // 2):
        for upwards in (True, False):
            at = c if upwards else c + CHUNKS // 2
            pass_on(upwards, opposite, half - 1, at).wait_recv()
            add([opposite], at, False)

    flat_out = out_ref.reshape(n_t * n_q * 2, n_lat)
    for t in range(n_t):
        for c in range(2):
            flat_out[pl.ds(t * n_q * 2 + c, n_q, stride=2), :] = total[t, c * n_q:(c + 1) * n_q, :]

    others = pl.ds(0, n_lat - 1)
    pltpu.make_async_copy(send_even.at[others], send_even.at[others], send1.at[0]).wait()
    pltpu.make_async_copy(send_odd.at[others], send_odd.at[others], send1.at[1]).wait()
    most = send_c.at[pl.ds(0, (n_lat - 1) * n_t), :]
    pltpu.make_async_copy(most, most, send2).wait()
    for sem in (send_up, send_down):
        for step in range(half):
            sent = gathered.at[0, pl.ds(0, n_t if step < half - 1 else n_t // 2)]
            pltpu.make_async_copy(sent, sent, sem.at[step]).wait()


def on_device(n_lat, n_rad, fourier, legendre, inverse, order_of_slot, degree_of_slot, degree_count):
    f, c, r, h, m, n_l = fourier.shape
    n_deg, n_h = legendre.shape[1:]
    n_t, n_q, full = inverse.shape
    half = n_rad // 2
    rows = jnp.transpose(fourier, (0, 1, 2, 5, 3, 4)).reshape(f * c * r, n_l, h, m)
    block = min(LANES, n_deg)
    any_space = pl.BlockSpec(memory_space=pl.ANY)
    in_vmem = pl.BlockSpec(memory_space=pltpu.VMEM)
    dma = pltpu.SemaphoreType.DMA
    pairs = (n_lat, n_l // 2, 2, LANES)
    return pl.pallas_call(
        functools.partial(kernel, (n_lat, n_rad, n_l, n_deg, n_t)),
        out_shape=jax.ShapeDtypeStruct((n_t, n_q, c, n_lat), F32),
        in_specs=[in_vmem] * 3 + [any_space] * 3,
        out_specs=in_vmem,
        scratch_shapes=[
            pltpu.VMEM((n_l, f * c * r, h, m), BF16),
            pltpu.VMEM((n_deg, n_h), BF16),
            pltpu.VMEM((n_t, n_q, full), BF16),
            pltpu.VMEM((n_lat * n_l, LANES), F32),
            pltpu.VMEM((n_lat * n_l, LANES), F32),
            pltpu.VMEM(pairs, BF16),
            pltpu.VMEM(pairs, BF16),
            pltpu.VMEM(pairs, BF16),
            pltpu.VMEM(pairs, BF16),
            pltpu.VMEM((n_deg, n_deg), BF16),
            pltpu.VMEM((n_deg, LANES), F32),
            pltpu.VMEM((n_deg, n_h), BF16),
            pltpu.VMEM((n_deg, LANES), BF16),
            pltpu.VMEM((n_lat * n_t, LANES), BF16),
            pltpu.VMEM((n_lat * n_t, LANES), F32),
            pltpu.VMEM((n_rad, n_t, n_lat, LANES), BF16),
            pltpu.VMEM((n_rad, n_t, c * n_q, LANES), BF16),
            pltpu.VMEM((n_t, c * n_q, n_lat), F32),
            dma((n_l,)), dma, dma,
            dma((2,)), dma((2,)), dma, dma,
            dma((half,)), dma((half,)), dma((half, CHUNKS)), dma((half, CHUNKS)),
        ],
        compiler_params=pltpu.CompilerParams(
            collective_id=0, has_side_effects=True, vmem_limit_bytes=56 << 20
        ),
    )(
        order_of_slot.reshape(1, n_lat),
        degree_of_slot.reshape(n_deg // block, block),
        degree_count.reshape(1, n_lat),
        rows,
        legendre.reshape(n_deg, n_h),
        inverse,
    )


def solution(mesh):
    in_specs = (
        P(None, None, "rad", None, None, "lat"),
        P("lat", None, None),
        P("lat", "rad", None),
        P(),
        P(),
        P(),
    )
    out_specs = P("lat", "rad", None, None)
    body = functools.partial(on_device, mesh.shape["lat"], mesh.shape["rad"])
    return jax.shard_map(
        body, mesh=mesh, in_specs=in_specs, out_specs=out_specs, check_vma=False
    )
```

```python
import functools

import jax
import jax.numpy as jnp
from jax import lax
from jax.experimental import pallas as pl
from jax.experimental.pallas import tpu as pltpu
from jax.sharding import PartitionSpec as P

BF16 = jnp.bfloat16
F32 = jnp.float32
MESH = pl.DeviceIdType.MESH
LANES = 128


def iota(shape, dim):
    return lax.broadcasted_iota(jnp.int32, shape, dim)


def column(row):
    return jnp.transpose(jnp.broadcast_to(row, (LANES, row.shape[1])))


def dot_nt(a, b):
    return lax.dot_general(a, b, (((1,), (1,)), ((), ())), preferred_element_type=F32)


def kernel(
    dims,
    order_ref, degree_ref, count_ref, rows_hbm, table_hbm, inverse_hbm,
    out_ref,
    rows, table, north, south, send_even, send_odd, recv_even, recv_odd,
    natural_degree, pick, column_degree, table_live, send_c, recv_c, wide,
    bring_c, got_c, matrices, right_side, send_o, recv_o,
    rows_sem, table_sem, send0, recv0, send1, recv1, send2, recv2, send3, recv3, send4, recv4,
):
    n_lat, n_rad, n_l, n_deg, n_t = dims
    own = n_t // n_rad
    n_q, full = matrices.shape[2], matrices.shape[3]
    radii = full // 2 // n_rad
    me = lax.axis_index("lat")
    y = lax.axis_index("rad")
    group = min(8, n_lat)
    planes = n_lat // group

    def load_rows(l):
        return pltpu.make_async_copy(rows_hbm.at[:, l], rows.at[l], rows_sem.at[l])

    for l in range(n_l):
        load_rows(l).start()
    load_table = pltpu.make_async_copy(table_hbm, table, table_sem)
    load_table.start()

    barrier = pltpu.get_barrier_semaphore()

    def greet_lat(k, carry):
        pl.semaphore_signal(
            barrier, inc=1, device_id={"lat": lax.rem(me + k, n_lat)}, device_id_type=MESH
        )
        return carry

    def greet_rad(k, carry):
        pl.semaphore_signal(
            barrier, inc=1, device_id={"rad": lax.rem(y + k, n_rad)}, device_id_type=MESH
        )
        return carry

    lax.fori_loop(1, n_lat, greet_lat, 0)
    lax.fori_loop(1, n_rad, greet_rad, 0)

    order = order_ref[...].astype(F32)
    order_column = column(order)[:, :n_lat]
    order_pick = jnp.where(
        order_column == iota((n_lat, n_lat), 1).astype(F32), 1.0, 0.0
    ).astype(BF16)
    for l in range(n_l):
        load_rows(l).wait()
        picked = dot_nt(order_pick, rows.at[l].reshape(2 * LANES, n_lat)[...])
        north[pl.ds(l, n_lat, stride=n_l), :] = picked[:, :LANES]
        south[pl.ds(l, n_lat, stride=n_l), :] = picked[:, LANES:]

    source, target = iota((2 * LANES, 2 * LANES), 0), iota((2 * LANES, 2 * LANES), 1)
    fold = jnp.where(
        source // 2 == target % LANES,
        jnp.where((source % 2 == 1) & (target >= LANES), -1.0, 1.0),
        0.0,
    ).astype(BF16)

    pl.semaphore_wait(barrier, n_lat + n_rad - 2)

    def send_matrices(k, carry):
        peer = lax.rem(y + k, n_rad)
        pltpu.make_async_remote_copy(
            src_ref=inverse_hbm.at[pl.ds(peer * own, own)], dst_ref=matrices.at[:, y],
            send_sem=send0, recv_sem=recv0,
            device_id={"rad": peer}, device_id_type=MESH,
        ).start()
        return carry

    lax.fori_loop(1, n_rad, send_matrices, 0)
    pltpu.make_async_copy(inverse_hbm.at[pl.ds(y * own, own)], matrices.at[:, y], recv0).start()

    def fold_and_send(k, carry):
        far = lax.select(lax.rem(k, 2) == 0, k // 2, lax.rem(planes - k // 2, planes))
        plane = lax.rem(me // group + far, planes)
        at = pl.ds(pl.multiple_of(plane * (group * n_l), 16), group * n_l)
        both = jnp.concatenate([north[at, :], south[at, :]], axis=1).astype(BF16)
        folded = jnp.dot(both, fold, preferred_element_type=F32).astype(BF16)
        send_even.reshape(n_lat * n_l, LANES)[at, :] = folded[:, :LANES]
        send_odd.reshape(n_lat * n_l, LANES)[at, :] = folded[:, LANES:]

        def send(i, c):
            peer = plane * group + lax.rem(me + i, group)

            @pl.when(peer != me)
            def _():
                for p, (src, dst) in enumerate(((send_even, recv_even), (send_odd, recv_odd))):
                    pltpu.make_async_remote_copy(
                        src_ref=src.at[peer], dst_ref=dst.at[me],
                        send_sem=send1.at[p], recv_sem=recv1.at[p],
                        device_id={"lat": peer}, device_id_type=MESH,
                    ).start()

            @pl.when(peer == me)
            def _():
                for p, (src, dst) in enumerate(((send_even, recv_even), (send_odd, recv_odd))):
                    pltpu.make_async_copy(src.at[me], dst.at[me], recv1.at[p]).start()

            return c

        return lax.fori_loop(0, group, send, carry)

    lax.fori_loop(1, planes + 1, fold_and_send, 0)

    mine = jnp.sum(jnp.where(iota((1, n_lat), 1) == me, order, 0.0), axis=1, keepdims=True)
    count = jnp.sum(
        jnp.where(iota((1, n_lat), 1).astype(F32) == mine, count_ref[...].astype(F32), 0.0),
        axis=1, keepdims=True,
    )
    first = n_deg - count
    blocks, block = degree_ref.shape

    def to_column(b, carry):
        at = pl.ds(pl.multiple_of(b * block, block), block)
        natural_degree[at, :] = column(degree_ref[pl.ds(b, 1), :].astype(F32))
        return carry

    lax.fori_loop(0, blocks, to_column, 0)
    step = n_deg // own // blocks

    for h in range(own):
        def pick_rows(b, carry):
            held = natural_degree[pl.ds(b * (step * own) + h, step, stride=own), :]
            at = pl.ds(pl.multiple_of(b * step + h * (n_deg // own), step), step)
            column_degree[at, :] = held
            for j in range(blocks):
                lane = (iota((step, block), 1) + j * block).astype(F32)
                cell = held[:, :block]
                pick[at, j * block:(j + 1) * block] = jnp.where(
                    (cell == lane) & (cell >= first), 1.0, 0.0
                ).astype(BF16)
            return carry

        lax.fori_loop(0, blocks, pick_rows, 0)

    load_table.wait()
    rows_at_once = min(256, n_deg // own)

    def order_rows(b, carry):
        at = pl.ds(pl.multiple_of(b * rows_at_once, rows_at_once), rows_at_once)
        table_live[at, :] = jnp.dot(
            pick[at, :], table[...], preferred_element_type=F32
        ).astype(BF16)
        return carry

    lax.fori_loop(0, n_deg // rows_at_once, order_rows, 0)

    pltpu.make_async_copy(recv_even, recv_even, recv1.at[0]).wait()
    pltpu.make_async_copy(recv_odd, recv_odd, recv1.at[1]).wait()

    parts = n_deg // own // rows_at_once
    peers = rows_at_once // n_rad

    for h in range(own):
        def analyse_and_send(k, carry):
            part = lax.rem(me // peers + k, parts)
            begin = pl.multiple_of(part * rows_at_once, rows_at_once)
            at = pl.ds(begin + h * (n_deg // own), rows_at_once)
            both = jnp.concatenate(
                [
                    recv_even.reshape(n_lat * n_l, LANES)[...],
                    recv_odd.reshape(n_lat * n_l, LANES)[...],
                ],
                axis=1,
            )
            product = jnp.dot(table_live[at, :], both, preferred_element_type=F32)
            parity = (column_degree[at, :] - first).astype(jnp.int32) & 1
            send_c.at[h].reshape(n_lat * n_rad, LANES)[pl.ds(begin, rows_at_once), :] = jnp.where(
                parity == 0, product[:, :LANES], product[:, LANES:]
            ).astype(BF16)

            def send(i, c):
                peer = part * peers + lax.rem(me + i, peers)
                src, dst = send_c.at[h, peer], recv_c.at[h, me]

                @pl.when(peer != me)
                def _():
                    pltpu.make_async_remote_copy(
                        src_ref=src, dst_ref=dst, send_sem=send2.at[h], recv_sem=recv2.at[h],
                        device_id={"lat": peer}, device_id_type=MESH,
                    ).start()

                @pl.when(peer == me)
                def _():
                    pltpu.make_async_copy(src, dst, recv2.at[h]).start()

                return c

            return lax.fori_loop(0, peers, send, carry)

        lax.fori_loop(0, parts, analyse_and_send, 0)

    for h in range(own):
        pltpu.make_async_copy(recv_c.at[h], recv_c.at[h], recv2.at[h]).wait()
        wide[h] = recv_c.at[h].reshape(n_lat * n_rad, LANES)[...].astype(F32)

        def bring(k, carry):
            peer = lax.rem(y + k, n_rad)
            bring_c[h, peer] = wide[h, pl.ds(peer, n_lat, stride=n_rad), :].astype(BF16)
            pltpu.make_async_remote_copy(
                src_ref=bring_c.at[h, peer], dst_ref=got_c.at[h, y],
                send_sem=send3.at[h], recv_sem=recv3.at[h],
                device_id={"rad": peer}, device_id_type=MESH,
            ).start()
            return carry

        lax.fori_loop(1, n_rad, bring, 0)
        got_c[h, y] = wide[h, pl.ds(y, n_lat, stride=n_rad), :].astype(BF16)

    pltpu.make_async_copy(matrices, matrices, recv0).wait()
    others = pl.ds(0, n_rad - 1)
    for h in range(own):
        pltpu.make_async_copy(got_c.at[h, others], got_c.at[h, others], recv3.at[h]).wait()
        for o in range(n_rad):
            turned = jnp.transpose(got_c[h, o].astype(F32))
            for f in range(2):
                pair = [turned[(2 * f + c) * radii:(2 * f + c + 1) * radii, :] for c in range(2)]
                right_side[h, f * (full // 2) + o * radii:f * (full // 2) + (o + 1) * radii, :] = (
                    jnp.concatenate(pair, axis=1).astype(BF16)
                )
        solved = jnp.dot(
            matrices.at[h].reshape(full, full)[...], right_side[h], preferred_element_type=F32
        ).astype(BF16)
        for o in range(n_rad):
            send_o[h, o] = solved[o * n_q:(o + 1) * n_q, :]

        def give(k, carry):
            peer = lax.rem(y + k, n_rad)
            pltpu.make_async_remote_copy(
                src_ref=send_o.at[h, peer], dst_ref=recv_o.at[h, y],
                send_sem=send4.at[h], recv_sem=recv4.at[h],
                device_id={"rad": peer}, device_id_type=MESH,
            ).start()
            return carry

        lax.fori_loop(1, n_rad, give, 0)
        recv_o[h, y] = send_o[h, y]

    flat_out = out_ref.reshape(n_t * n_q * 2, n_lat)
    for h in range(own):
        pltpu.make_async_copy(recv_o.at[h, others], recv_o.at[h, others], recv4.at[h]).wait()
        for o in range(n_rad):
            block_o = recv_o[h, o].astype(F32)
            for c in range(2):
                flat_out[pl.ds((o * own + h) * n_q * 2 + c, n_q, stride=2), :] = block_o[
                    :, c * n_lat:(c + 1) * n_lat
                ]

    left = inverse_hbm.at[pl.ds(0, (n_rad - 1) * own)]
    pltpu.make_async_copy(left, left, send0).wait()
    most = pl.ds(0, n_lat - 1)
    pltpu.make_async_copy(send_even.at[most], send_even.at[most], send1.at[0]).wait()
    pltpu.make_async_copy(send_odd.at[most], send_odd.at[most], send1.at[1]).wait()
    for h in range(own):
        pltpu.make_async_copy(send_c.at[h, most], send_c.at[h, most], send2.at[h]).wait()
        pltpu.make_async_copy(bring_c.at[h, others], bring_c.at[h, others], send3.at[h]).wait()
        pltpu.make_async_copy(send_o.at[h, others], send_o.at[h, others], send4.at[h]).wait()


def on_device(n_lat, n_rad, fourier, legendre, inverse, order_of_slot, degree_of_slot, degree_count):
    f, c, r, h, m, n_l = fourier.shape
    n_deg, n_h = legendre.shape[1:]
    n_t, n_q, full = inverse.shape
    own = n_t // n_rad
    rows = jnp.transpose(fourier, (0, 1, 2, 5, 3, 4)).reshape(f * c * r, n_l, h, m)
    block = min(LANES, n_deg)
    any_space = pl.BlockSpec(memory_space=pl.ANY)
    in_vmem = pl.BlockSpec(memory_space=pltpu.VMEM)
    dma = pltpu.SemaphoreType.DMA
    pairs = (n_lat, n_l // 2, 2, LANES)
    return pl.pallas_call(
        functools.partial(kernel, (n_lat, n_rad, n_l, n_deg, n_t)),
        out_shape=jax.ShapeDtypeStruct((n_t, n_q, c, n_lat), F32),
        in_specs=[in_vmem] * 3 + [any_space] * 3,
        out_specs=in_vmem,
        scratch_shapes=[
            pltpu.VMEM((n_l, f * c * r, h, m), BF16),
            pltpu.VMEM((n_deg, n_h), BF16),
            pltpu.VMEM((n_lat * n_l, LANES), F32),
            pltpu.VMEM((n_lat * n_l, LANES), F32),
            pltpu.VMEM(pairs, BF16),
            pltpu.VMEM(pairs, BF16),
            pltpu.VMEM(pairs, BF16),
            pltpu.VMEM(pairs, BF16),
            pltpu.VMEM((n_deg, LANES), F32),
            pltpu.VMEM((n_deg, n_deg), BF16),
            pltpu.VMEM((n_deg, LANES), F32),
            pltpu.VMEM((n_deg, n_h), BF16),
            pltpu.VMEM((own, n_lat, n_rad, LANES), BF16),
            pltpu.VMEM((own, n_lat, n_rad, LANES), BF16),
            pltpu.VMEM((own, n_lat * n_rad, LANES), F32),
            pltpu.VMEM((own, n_rad, n_lat, LANES), BF16),
            pltpu.VMEM((own, n_rad, n_lat, LANES), BF16),
            pltpu.VMEM((own, n_rad, n_q, full), BF16),
            pltpu.VMEM((own, full, c * n_lat), BF16),
            pltpu.VMEM((own, n_rad, n_q, c * n_lat), BF16),
            pltpu.VMEM((own, n_rad, n_q, c * n_lat), BF16),
            dma((n_l,)), dma, dma, dma,
            dma((2,)), dma((2,)), dma((own,)), dma((own,)),
            dma((own,)), dma((own,)), dma((own,)), dma((own,)),
        ],
        compiler_params=pltpu.CompilerParams(
            collective_id=0, has_side_effects=True, vmem_limit_bytes=56 << 20
        ),
    )(
        order_of_slot.reshape(1, n_lat),
        degree_of_slot.reshape(n_deg // block, block),
        degree_count.reshape(1, n_lat),
        rows,
        legendre.reshape(n_deg, n_h),
        inverse,
    )


def solution(mesh):
    in_specs = (
        P(None, None, "rad", None, None, "lat"),
        P("lat", None, None),
        P("lat", "rad", None),
        P(),
        P(),
        P(),
    )
    out_specs = P("lat", "rad", None, None)
    body = functools.partial(on_device, mesh.shape["lat"], mesh.shape["rad"])
    return jax.shard_map(
        body, mesh=mesh, in_specs=in_specs, out_specs=out_specs, check_vma=False
    )
```

```python
import functools

import jax
import jax.numpy as jnp
from jax import lax
from jax.experimental import pallas as pl
from jax.experimental.pallas import tpu as pltpu
from jax.sharding import PartitionSpec as P

BF16 = jnp.bfloat16
F32 = jnp.float32
MESH = pl.DeviceIdType.MESH
LANES = 128


def iota(shape, dim):
    return lax.broadcasted_iota(jnp.int32, shape, dim)


def column(row):
    return jnp.transpose(jnp.broadcast_to(row, (LANES, row.shape[1])))


def dot_nt(a, b):
    return lax.dot_general(a, b, (((1,), (1,)), ((), ())), preferred_element_type=F32)


def farthest_first(k, n):
    return n // 2 + lax.select(lax.rem(k, 2) == 0, k // 2, -((k + 1) // 2))


def kernel(
    dims,
    order_hbm, degree_hbm, count_hbm, rows_hbm, table_hbm, inverse_hbm,
    recv_o,
    order_ref, degree_ref, count_ref, rows, table, north, south, send_folds, recv_folds,
    pick, column_degree, table_live, send_c, got_c, wide, matrices, right_side, send_o,
    small_sem, rows_sem, table_sem, send0, recv0, send1, recv1, send2, recv2, send4, recv4,
):
    n_lat, n_rad, n_l, n_deg, n_t = dims
    own = n_t // n_rad
    n_q, full = matrices.shape[2], matrices.shape[3]
    radii = full // 2 // n_rad
    me = lax.axis_index("lat")
    y = lax.axis_index("rad")
    group, planes = 8, n_lat // 8
    z, x, core = me // group, lax.rem(me, group) // 2, lax.rem(me, 2)
    places = [
        lax.rem(x + d, 4) * 2 + lax.rem(core + 1 + i, 2) for d in (2, 1, 3, 0) for i in range(2)
    ]

    def ring_of_planes(k):
        return lax.rem(z + farthest_first(k, planes), planes)

    def rad_peer(k):
        return lax.rem(y + farthest_first(k, n_rad), n_rad)

    smalls = [
        pltpu.make_async_copy(src, dst, small_sem.at[i])
        for i, (src, dst) in enumerate(
            ((order_hbm, order_ref), (degree_hbm, degree_ref), (count_hbm, count_ref))
        )
    ]

    def load_rows(l):
        return pltpu.make_async_copy(rows_hbm.at[:, l], rows.at[l], rows_sem.at[l])

    smalls[0].start()
    for l in range(n_l):
        load_rows(l).start()
    smalls[1].start()
    smalls[2].start()
    load_table = pltpu.make_async_copy(table_hbm, table, table_sem)
    load_table.start()

    barrier = pltpu.get_barrier_semaphore()

    def greet_lat(k, carry):
        plane = ring_of_planes(k)
        for place in places:
            pl.semaphore_signal(
                barrier, inc=1, device_id={"lat": plane * group + place}, device_id_type=MESH
            )
        return carry

    def greet_rad(k, carry):
        pl.semaphore_signal(
            barrier, inc=1, device_id={"rad": lax.rem(y + k, n_rad)}, device_id_type=MESH
        )
        return carry

    lax.fori_loop(0, planes - 1, greet_lat, 0)
    for place in places[:-1]:
        pl.semaphore_signal(
            barrier, inc=1, device_id={"lat": z * group + place}, device_id_type=MESH
        )
    lax.fori_loop(1, n_rad, greet_rad, 0)

    smalls[0].wait()
    order = order_ref[...].astype(F32)
    order_column = column(order)[:, :n_lat]
    order_pick = jnp.where(
        order_column == iota((n_lat, n_lat), 1).astype(F32), 1.0, 0.0
    ).astype(BF16)
    load_rows(0).wait()
    for l in range(1, n_l):
        load_rows(l).wait()
    for l in range(n_l):
        picked = dot_nt(order_pick, rows.at[l].reshape(2 * LANES, n_lat)[...])
        north[pl.ds(l, n_lat, stride=n_l), :] = picked[:, :LANES]
        south[pl.ds(l, n_lat, stride=n_l), :] = picked[:, LANES:]

    source, target = iota((2 * LANES, 2 * LANES), 0), iota((2 * LANES, 2 * LANES), 1)
    fold = jnp.where(
        source // 2 == target % LANES,
        jnp.where((source % 2 == 1) & (target >= LANES), -1.0, 1.0),
        0.0,
    ).astype(BF16)

    pl.semaphore_wait(barrier, n_lat + n_rad - 2)

    def send_matrices(k, carry):
        peer = rad_peer(k)
        pltpu.make_async_remote_copy(
            src_ref=inverse_hbm.at[pl.ds(peer * own, own)], dst_ref=matrices.at[:, y],
            send_sem=send0, recv_sem=recv0,
            device_id={"rad": peer}, device_id_type=MESH,
        ).start()
        return carry

    lax.fori_loop(0, n_rad - 1, send_matrices, 0)
    pltpu.make_async_copy(inverse_hbm.at[pl.ds(y * own, own)], matrices.at[:, y], recv0).start()

    def fold_and_send(plane, own_plane):
        at = pl.ds(pl.multiple_of(plane * (group * n_l), 16), group * n_l)
        both = jnp.concatenate([north[at, :], south[at, :]], axis=1).astype(BF16)
        folded = jnp.dot(both, fold, preferred_element_type=F32).astype(BF16)
        for p in range(2):
            send_folds.at[p].reshape(n_lat * n_l, LANES)[at, :] = folded[
                :, p * LANES:(p + 1) * LANES
            ]
        for place in places[:-1] if own_plane else places:
            peer = plane * group + place
            pltpu.make_async_remote_copy(
                src_ref=send_folds.at[:, peer], dst_ref=recv_folds.at[:, me],
                send_sem=send1, recv_sem=recv1,
                device_id={"lat": peer}, device_id_type=MESH,
            ).start()
        if own_plane:
            pltpu.make_async_copy(send_folds.at[:, me], recv_folds.at[:, me], recv1).start()

    def fold_other(k, carry):
        fold_and_send(ring_of_planes(k), False)
        return carry

    lax.fori_loop(0, planes - 1, fold_other, 0)
    fold_and_send(z, True)

    smalls[1].wait()
    smalls[2].wait()
    mine = jnp.sum(jnp.where(iota((1, n_lat), 1) == me, order, 0.0), axis=1, keepdims=True)
    count = jnp.sum(
        jnp.where(iota((1, n_lat), 1).astype(F32) == mine, count_ref[...].astype(F32), 0.0),
        axis=1, keepdims=True,
    )
    first = n_deg - count
    blocks, block = degree_ref.shape

    def pick_rows(b, carry):
        at = pl.ds(pl.multiple_of(b * block, block), block)
        held = column(degree_ref[pl.ds(b, 1), :].astype(F32))
        column_degree[at, :] = held
        cell = held[:, :block]
        for j in range(blocks):
            lane = (iota((block, block), 1) + j * block).astype(F32)
            pick[at, j * block:(j + 1) * block] = jnp.where(
                (cell == lane) & (cell >= first), 1.0, 0.0
            ).astype(BF16)
        return carry

    lax.fori_loop(0, blocks, pick_rows, 0)

    load_table.wait()
    rows_at_once = 2 * group * n_t

    def order_rows(b, carry):
        at = pl.ds(pl.multiple_of(b * rows_at_once, rows_at_once), rows_at_once)
        table_live[at, :] = jnp.dot(
            pick[at, :], table[...], preferred_element_type=F32
        ).astype(BF16)
        return carry

    lax.fori_loop(0, n_deg // rows_at_once, order_rows, 0)

    pltpu.make_async_copy(recv_folds, recv_folds, recv1).wait()

    def analyse(pair):
        at = pl.ds(pl.multiple_of(pair * rows_at_once, rows_at_once), rows_at_once)
        both = jnp.concatenate(
            [recv_folds.at[p].reshape(n_lat * n_l, LANES)[...] for p in range(2)], axis=1
        )
        product = jnp.dot(table_live[at, :], both, preferred_element_type=F32)
        parity = (column_degree[at, :] - first).astype(jnp.int32) & 1
        send_c.reshape(n_deg, LANES)[at, :] = jnp.where(
            parity == 0, product[:, :LANES], product[:, LANES:]
        ).astype(BF16)

    def send(peer, peer_y):
        pltpu.make_async_remote_copy(
            src_ref=send_c.at[peer, peer_y], dst_ref=got_c.at[y, me],
            send_sem=send2, recv_sem=recv2,
            device_id={"lat": peer, "rad": peer_y}, device_id_type=MESH,
        ).start()

    def send_pair(k, carry):
        pair = lax.rem(z // 2 + farthest_first(k, planes // 2), planes // 2)
        analyse(pair)

        def send_to(i, c):
            plane = pair * 2 + lax.rem(z + 1 + i // n_rad, 2)
            peer_y = rad_peer(lax.rem(i, n_rad))
            for place in places[:-1]:
                send(plane * group + place, peer_y)
            last = plane * group + places[-1]

            @pl.when((last != me) | (peer_y != y))
            def _():
                send(last, peer_y)

            return c

        lax.fori_loop(0, 2 * n_rad, send_to, 0)
        return carry

    lax.fori_loop(0, planes // 2, send_pair, 0)
    pltpu.make_async_copy(send_c.at[me, y], got_c.at[y, me], recv2).start()

    pltpu.make_async_copy(matrices, matrices, recv0).wait()
    pltpu.make_async_copy(got_c, got_c, recv2).wait()
    for o in range(n_rad):
        wide[o] = got_c.at[o].reshape(n_lat * own, LANES)[...].astype(F32)
    for h in range(own):
        for o in range(n_rad):
            turned = jnp.transpose(wide[o, pl.ds(h, n_lat, stride=own), :])
            for f in range(2):
                pair = [turned[(2 * f + c) * radii:(2 * f + c + 1) * radii, :] for c in range(2)]
                right_side[h, f * (full // 2) + o * radii:f * (full // 2) + (o + 1) * radii, :] = (
                    jnp.concatenate(pair, axis=1).astype(BF16)
                )
        solved = jnp.dot(
            matrices.at[h].reshape(full, full)[...], right_side[h], preferred_element_type=F32
        ).astype(BF16)
        for o in range(n_rad):
            send_o[h, o] = solved[o * n_q:(o + 1) * n_q, :]

        def give(k, carry):
            peer = rad_peer(k)
            pltpu.make_async_remote_copy(
                src_ref=send_o.at[h, peer], dst_ref=recv_o.at[h, y],
                send_sem=send4.at[h], recv_sem=recv4.at[h],
                device_id={"rad": peer}, device_id_type=MESH,
            ).start()
            return carry

        lax.fori_loop(0, n_rad - 1, give, 0)
        pltpu.make_async_copy(send_o.at[h, y], recv_o.at[h, y], recv4.at[h]).start()

    for h in range(own):
        pltpu.make_async_copy(recv_o.at[h], recv_o.at[h], recv4.at[h]).wait()

    left = inverse_hbm.at[pl.ds(0, (n_rad - 1) * own)]
    pltpu.make_async_copy(left, left, send0).wait()
    most = pl.ds(0, n_lat - 1)
    pltpu.make_async_copy(send_folds.at[:, most], send_folds.at[:, most], send1).wait()
    pltpu.make_async_copy(send_c.at[most], send_c.at[most], send2).wait()
    rest, others = send_c.at[0, pl.ds(0, n_rad - 1)], pl.ds(0, n_rad - 1)
    pltpu.make_async_copy(rest, rest, send2).wait()
    for h in range(own):
        pltpu.make_async_copy(send_o.at[h, others], send_o.at[h, others], send4.at[h]).wait()


def widen(solved_ref, out_ref):
    n_rad, n_q = solved_ref.shape[1:3]
    n_lat = out_ref.shape[4]
    for o in range(n_rad):
        flat = out_ref.at[o, 0].reshape(n_q * 2, n_lat)
        block = solved_ref[0, o].astype(F32)
        for c in range(2):
            flat[pl.ds(c, n_q, stride=2), :] = block[:, c * n_lat:(c + 1) * n_lat]


def on_device(n_lat, n_rad, fourier, legendre, inverse, order_of_slot, degree_of_slot, degree_count):
    f, c, r, h, m, n_l = fourier.shape
    n_deg, n_h = legendre.shape[1:]
    n_t, n_q, full = inverse.shape
    own = n_t // n_rad
    rows = jnp.transpose(fourier, (0, 1, 2, 5, 3, 4)).reshape(f * c * r, n_l, h, m)
    block = min(LANES, n_deg)
    any_space = pl.BlockSpec(memory_space=pl.ANY)
    dma = pltpu.SemaphoreType.DMA
    pairs = (2, n_lat, n_l // 2, 2, LANES)
    solved = pl.pallas_call(
        functools.partial(kernel, (n_lat, n_rad, n_l, n_deg, n_t)),
        out_shape=jax.ShapeDtypeStruct((own, n_rad, n_q, c * n_lat), BF16),
        in_specs=[any_space] * 6,
        out_specs=any_space,
        scratch_shapes=[
            pltpu.VMEM((1, n_lat), jnp.int32),
            pltpu.VMEM((n_deg // block, block), jnp.int32),
            pltpu.VMEM((1, n_lat), jnp.int32),
            pltpu.VMEM((n_l, f * c * r, h, m), BF16),
            pltpu.VMEM((n_deg, n_h), BF16),
            pltpu.VMEM((n_lat * n_l, LANES), F32),
            pltpu.VMEM((n_lat * n_l, LANES), F32),
            pltpu.VMEM(pairs, BF16),
            pltpu.VMEM(pairs, BF16),
            pltpu.VMEM((n_deg, n_deg), BF16),
            pltpu.VMEM((n_deg, LANES), F32),
            pltpu.VMEM((n_deg, n_h), BF16),
            pltpu.VMEM((n_lat, n_rad, own, LANES), BF16),
            pltpu.VMEM((n_rad, n_lat, own, LANES), BF16),
            pltpu.VMEM((n_rad, n_lat * own, LANES), F32),
            pltpu.VMEM((own, n_rad, n_q, full), BF16),
            pltpu.VMEM((own, full, c * n_lat), BF16),
            pltpu.VMEM((own, n_rad, n_q, c * n_lat), BF16),
            dma((3,)), dma((n_l,)), dma, dma, dma,
            dma, dma, dma, dma, dma((own,)), dma((own,)),
        ],
        compiler_params=pltpu.CompilerParams(
            collective_id=0, has_side_effects=True, vmem_limit_bytes=56 << 20
        ),
    )(
        order_of_slot.reshape(1, n_lat),
        degree_of_slot.reshape(n_deg // block, block),
        degree_count.reshape(1, n_lat),
        rows,
        legendre.reshape(n_deg, n_h),
        inverse,
    )
    return pl.pallas_call(
        widen,
        grid=(own,),
        out_shape=jax.ShapeDtypeStruct((n_rad, own, n_q, c, n_lat), F32),
        in_specs=[pl.BlockSpec((1, n_rad, n_q, c * n_lat), lambda i: (i, 0, 0, 0))],
        out_specs=pl.BlockSpec((n_rad, 1, n_q, c, n_lat), lambda i: (0, i, 0, 0, 0)),
    )(solved).reshape(n_t, n_q, c, n_lat)


def solution(mesh):
    in_specs = (
        P(None, None, "rad", None, None, "lat"),
        P("lat", None, None),
        P("lat", "rad", None),
        P(),
        P(),
        P(),
    )
    out_specs = P("lat", "rad", None, None)
    body = functools.partial(on_device, mesh.shape["lat"], mesh.shape["rad"])
    return jax.shard_map(
        body, mesh=mesh, in_specs=in_specs, out_specs=out_specs, check_vma=False
    )
```

```python
import functools

import jax
import jax.numpy as jnp
from jax import lax
from jax.experimental import pallas as pl
from jax.experimental.pallas import tpu as pltpu
from jax.sharding import PartitionSpec as P

BF16 = jnp.bfloat16
F32 = jnp.float32
MESH = pl.DeviceIdType.MESH
LANES = 128
PIECES = 2


def iota(shape, dim):
    return lax.broadcasted_iota(jnp.int32, shape, dim)


def column(row):
    return jnp.transpose(jnp.broadcast_to(row, (LANES, row.shape[1])))


def dot_nt(a, b):
    return lax.dot_general(a, b, (((1,), (1,)), ((), ())), preferred_element_type=F32)


def farthest_first(k, n):
    return n // 2 + lax.select(lax.rem(k, 2) == 0, k // 2, -((k + 1) // 2))


def kernel(
    dims,
    order_hbm, degree_hbm, count_hbm, rows_hbm, table_hbm, inverse_hbm,
    recv_o,
    order_ref, degree_ref, count_ref, rows, table, north, south, send_folds, recv_folds,
    natural_degree, pick, column_degree, table_live, send_c, recv_c, wide,
    bring_c, got_c, matrices, right_side, send_o,
    small_sem, rows_sem, table_sem, send0, recv0, send1, recv1, send2, recv2, send3, recv3, send4, recv4,
):
    n_lat, n_rad, n_l, n_deg, n_t = dims
    own = n_t // n_rad
    n_q, full = matrices.shape[2], matrices.shape[3]
    radii = full // 2 // n_rad
    me = lax.axis_index("lat")
    y = lax.axis_index("rad")
    group, planes = 8, n_lat // 8
    z, x, core = me // group, lax.rem(me, group) // 2, lax.rem(me, 2)
    places = [
        lax.rem(x + d, 4) * 2 + lax.rem(core + 1 + i, 2) for d in (2, 1, 3, 0) for i in range(2)
    ]

    def ring_of_planes(k):
        return lax.rem(z + farthest_first(k, planes), planes)

    def rad_peer(k):
        return lax.rem(y + farthest_first(k, n_rad), n_rad)

    smalls = [
        pltpu.make_async_copy(src, dst, small_sem.at[i])
        for i, (src, dst) in enumerate(
            ((order_hbm, order_ref), (degree_hbm, degree_ref), (count_hbm, count_ref))
        )
    ]

    def load_rows(l):
        return pltpu.make_async_copy(rows_hbm.at[:, l], rows.at[l], rows_sem.at[l])

    smalls[0].start()
    for l in range(n_l):
        load_rows(l).start()
    smalls[1].start()
    smalls[2].start()
    load_table = pltpu.make_async_copy(table_hbm, table, table_sem)
    load_table.start()

    barrier = pltpu.get_barrier_semaphore()

    def greet_lat(k, carry):
        plane = ring_of_planes(k)
        for place in places:
            pl.semaphore_signal(
                barrier, inc=1, device_id={"lat": plane * group + place}, device_id_type=MESH
            )
        return carry

    def greet_rad(k, carry):
        pl.semaphore_signal(
            barrier, inc=1, device_id={"rad": lax.rem(y + k, n_rad)}, device_id_type=MESH
        )
        return carry

    lax.fori_loop(0, planes - 1, greet_lat, 0)
    for place in places[:-1]:
        pl.semaphore_signal(
            barrier, inc=1, device_id={"lat": z * group + place}, device_id_type=MESH
        )
    lax.fori_loop(1, n_rad, greet_rad, 0)

    smalls[0].wait()
    order = order_ref[...].astype(F32)
    order_column = column(order)[:, :n_lat]
    order_pick = jnp.where(
        order_column == iota((n_lat, n_lat), 1).astype(F32), 1.0, 0.0
    ).astype(BF16)
    load_rows(0).wait()
    for l in range(1, n_l):
        load_rows(l).wait()
    for l in range(n_l):
        picked = dot_nt(order_pick, rows.at[l].reshape(2 * LANES, n_lat)[...])
        north[pl.ds(l, n_lat, stride=n_l), :] = picked[:, :LANES]
        south[pl.ds(l, n_lat, stride=n_l), :] = picked[:, LANES:]

    source, target = iota((2 * LANES, 2 * LANES), 0), iota((2 * LANES, 2 * LANES), 1)
    fold = jnp.where(
        source // 2 == target % LANES,
        jnp.where((source % 2 == 1) & (target >= LANES), -1.0, 1.0),
        0.0,
    ).astype(BF16)

    pl.semaphore_wait(barrier, n_lat + n_rad - 2)

    def send_matrices(k, carry):
        peer = rad_peer(k)
        pltpu.make_async_remote_copy(
            src_ref=inverse_hbm.at[pl.ds(peer * own, own)], dst_ref=matrices.at[:, y],
            send_sem=send0, recv_sem=recv0,
            device_id={"rad": peer}, device_id_type=MESH,
        ).start()
        return carry

    lax.fori_loop(0, n_rad - 1, send_matrices, 0)
    pltpu.make_async_copy(inverse_hbm.at[pl.ds(y * own, own)], matrices.at[:, y], recv0).start()

    def fold_and_send(plane, own_plane):
        at = pl.ds(pl.multiple_of(plane * (group * n_l), 16), group * n_l)
        both = jnp.concatenate([north[at, :], south[at, :]], axis=1).astype(BF16)
        folded = jnp.dot(both, fold, preferred_element_type=F32).astype(BF16)
        for p in range(2):
            send_folds.at[p].reshape(n_lat * n_l, LANES)[at, :] = folded[
                :, p * LANES:(p + 1) * LANES
            ]
        for place in places[:-1] if own_plane else places:
            peer = plane * group + place
            pltpu.make_async_remote_copy(
                src_ref=send_folds.at[:, peer], dst_ref=recv_folds.at[:, me],
                send_sem=send1, recv_sem=recv1,
                device_id={"lat": peer}, device_id_type=MESH,
            ).start()
        if own_plane:
            pltpu.make_async_copy(send_folds.at[:, me], recv_folds.at[:, me], recv1).start()

    def fold_other(k, carry):
        fold_and_send(ring_of_planes(k), False)
        return carry

    lax.fori_loop(0, planes - 1, fold_other, 0)
    fold_and_send(z, True)

    smalls[1].wait()
    smalls[2].wait()
    mine = jnp.sum(jnp.where(iota((1, n_lat), 1) == me, order, 0.0), axis=1, keepdims=True)
    count = jnp.sum(
        jnp.where(iota((1, n_lat), 1).astype(F32) == mine, count_ref[...].astype(F32), 0.0),
        axis=1, keepdims=True,
    )
    first = n_deg - count
    blocks, block = degree_ref.shape

    def to_column(b, carry):
        at = pl.ds(pl.multiple_of(b * block, block), block)
        natural_degree[at, :] = column(degree_ref[pl.ds(b, 1), :].astype(F32))
        return carry

    lax.fori_loop(0, blocks, to_column, 0)
    step = n_deg // own // blocks

    for h in range(own):
        def pick_rows(b, carry):
            held = natural_degree[pl.ds(b * (step * own) + h, step, stride=own), :]
            at = pl.ds(pl.multiple_of(b * step + h * (n_deg // own), step), step)
            column_degree[at, :] = held
            for j in range(blocks):
                lane = (iota((step, block), 1) + j * block).astype(F32)
                cell = held[:, :block]
                pick[at, j * block:(j + 1) * block] = jnp.where(
                    (cell == lane) & (cell >= first), 1.0, 0.0
                ).astype(BF16)
            return carry

        lax.fori_loop(0, blocks, pick_rows, 0)

    load_table.wait()
    rows_at_once = min(256, n_deg // own)

    def order_rows(b, carry):
        at = pl.ds(pl.multiple_of(b * rows_at_once, rows_at_once), rows_at_once)
        table_live[at, :] = jnp.dot(
            pick[at, :], table[...], preferred_element_type=F32
        ).astype(BF16)
        return carry

    lax.fori_loop(0, n_deg // rows_at_once, order_rows, 0)

    pltpu.make_async_copy(recv_folds, recv_folds, recv1).wait()

    parts = n_deg // own // rows_at_once

    reach = planes // parts

    for h in range(own):
        def send(peer):
            pltpu.make_async_remote_copy(
                src_ref=send_c.at[h, peer], dst_ref=recv_c.at[h, me],
                send_sem=send2.at[h], recv_sem=recv2.at[h],
                device_id={"lat": peer}, device_id_type=MESH,
            ).start()

        def analyse_and_send(k, carry):
            part = lax.rem(z // reach + 1 + k, parts)
            begin = pl.multiple_of(part * rows_at_once, rows_at_once)
            at = pl.ds(begin + h * (n_deg // own), rows_at_once)
            both = jnp.concatenate(
                [recv_folds.at[p].reshape(n_lat * n_l, LANES)[...] for p in range(2)], axis=1
            )
            product = jnp.dot(table_live[at, :], both, preferred_element_type=F32)
            parity = (column_degree[at, :] - first).astype(jnp.int32) & 1
            send_c.at[h].reshape(n_lat * n_rad, LANES)[pl.ds(begin, rows_at_once), :] = jnp.where(
                parity == 0, product[:, :LANES], product[:, LANES:]
            ).astype(BF16)

            def send_plane(j, c):
                plane = part * reach + lax.rem(z + 1 + j, reach)
                for place in places[:-1]:
                    send(plane * group + place)
                last = plane * group + places[-1]

                @pl.when(last != me)
                def _():
                    send(last)

                return c

            return lax.fori_loop(0, reach, send_plane, carry)

        lax.fori_loop(0, parts, analyse_and_send, 0)
        pltpu.make_async_copy(send_c.at[h, me], recv_c.at[h, me], recv2.at[h]).start()

    some = n_lat // PIECES
    for h in range(own):
        pltpu.make_async_copy(recv_c.at[h], recv_c.at[h], recv2.at[h]).wait()
        wide[h] = recv_c.at[h].reshape(n_lat * n_rad, LANES)[...].astype(F32)
        for p in range(PIECES):
            def bring(k, carry):
                peer = rad_peer(k)
                bring_c[h, p, peer] = wide[
                    h, pl.ds(p * some * n_rad + peer, some, stride=n_rad), :
                ].astype(BF16)
                pltpu.make_async_remote_copy(
                    src_ref=bring_c.at[h, p, peer], dst_ref=got_c.at[h, p, y],
                    send_sem=send3.at[h, p], recv_sem=recv3.at[h, p],
                    device_id={"rad": peer}, device_id_type=MESH,
                ).start()
                return carry

            lax.fori_loop(0, n_rad - 1, bring, 0)
            got_c[h, p, y] = wide[
                h, pl.ds(p * some * n_rad + y, some, stride=n_rad), :
            ].astype(BF16)

    pltpu.make_async_copy(matrices, matrices, recv0).wait()
    others = pl.ds(0, n_rad - 1)
    slab = n_q // PIECES
    for h in range(own):
        for p in range(PIECES):
            pltpu.make_async_copy(
                got_c.at[h, p, others], got_c.at[h, p, others], recv3.at[h, p]
            ).wait()
            for o in range(n_rad):
                turned = jnp.transpose(got_c[h, p, o].astype(F32))
                for f in range(2):
                    pair = [
                        turned[(2 * f + c) * radii:(2 * f + c + 1) * radii, :] for c in range(2)
                    ]
                    begin = f * (full // 2) + o * radii
                    right_side[h, p, begin:begin + radii, :] = jnp.concatenate(
                        pair, axis=1
                    ).astype(BF16)
            solved = jnp.dot(
                matrices.at[h].reshape(full, full)[...], right_side[h, p],
                preferred_element_type=F32,
            )
            for o in range(n_rad):
                send_o[h, p, o] = jnp.concatenate(
                    [
                        solved[o * n_q + i * slab:o * n_q + (i + 1) * slab, :]
                        for i in range(PIECES)
                    ],
                    axis=1,
                ).astype(BF16)

            def give(k, carry):
                peer = rad_peer(k)
                pltpu.make_async_remote_copy(
                    src_ref=send_o.at[h, p, peer], dst_ref=recv_o.at[h, p, y],
                    send_sem=send4.at[h, p], recv_sem=recv4.at[h, p],
                    device_id={"rad": peer}, device_id_type=MESH,
                ).start()
                return carry

            lax.fori_loop(0, n_rad - 1, give, 0)
            pltpu.make_async_copy(
                send_o.at[h, p, y], recv_o.at[h, p, y], recv4.at[h, p]
            ).start()

    for h in range(own):
        for p in range(PIECES):
            pltpu.make_async_copy(recv_o.at[h, p], recv_o.at[h, p], recv4.at[h, p]).wait()

    left = inverse_hbm.at[pl.ds(0, (n_rad - 1) * own)]
    pltpu.make_async_copy(left, left, send0).wait()
    most = pl.ds(0, n_lat - 1)
    pltpu.make_async_copy(send_folds.at[:, most], send_folds.at[:, most], send1).wait()
    for h in range(own):
        pltpu.make_async_copy(send_c.at[h, most], send_c.at[h, most], send2.at[h]).wait()
        for p in range(PIECES):
            sent = bring_c.at[h, p, others]
            pltpu.make_async_copy(sent, sent, send3.at[h, p]).wait()
            sent = send_o.at[h, p, others]
            pltpu.make_async_copy(sent, sent, send4.at[h, p]).wait()


def widen(solved_ref, out_ref):
    n_rad, slab = solved_ref.shape[2:4]
    n_q, n_c, n_lat = out_ref.shape[2:]
    some = n_lat // PIECES
    for o in range(n_rad):
        flat = out_ref.at[o, 0].reshape(n_q * n_c, n_lat)
        block = [solved_ref[0, p, o].astype(F32) for p in range(PIECES)]
        for i in range(PIECES):
            for c in range(n_c):
                begin = (i * n_c + c) * some
                flat[pl.ds(i * slab * n_c + c, slab, stride=n_c), :] = jnp.concatenate(
                    [b[:, begin:begin + some] for b in block], axis=1
                )


def on_device(n_lat, n_rad, fourier, legendre, inverse, order_of_slot, degree_of_slot, degree_count):
    f, c, r, h, m, n_l = fourier.shape
    n_deg, n_h = legendre.shape[1:]
    n_t, n_q, full = inverse.shape
    own = n_t // n_rad
    rows = jnp.transpose(fourier, (0, 1, 2, 5, 3, 4)).reshape(f * c * r, n_l, h, m)
    block = min(LANES, n_deg)
    any_space = pl.BlockSpec(memory_space=pl.ANY)
    dma = pltpu.SemaphoreType.DMA
    pairs = (2, n_lat, n_l // 2, 2, LANES)
    solved = pl.pallas_call(
        functools.partial(kernel, (n_lat, n_rad, n_l, n_deg, n_t)),
        out_shape=jax.ShapeDtypeStruct((own, PIECES, n_rad, n_q // PIECES, c * n_lat), BF16),
        in_specs=[any_space] * 6,
        out_specs=any_space,
        scratch_shapes=[
            pltpu.VMEM((1, n_lat), jnp.int32),
            pltpu.VMEM((n_deg // block, block), jnp.int32),
            pltpu.VMEM((1, n_lat), jnp.int32),
            pltpu.VMEM((n_l, f * c * r, h, m), BF16),
            pltpu.VMEM((n_deg, n_h), BF16),
            pltpu.VMEM((n_lat * n_l, LANES), F32),
            pltpu.VMEM((n_lat * n_l, LANES), F32),
            pltpu.VMEM(pairs, BF16),
            pltpu.VMEM(pairs, BF16),
            pltpu.VMEM((n_deg, LANES), F32),
            pltpu.VMEM((n_deg, n_deg), BF16),
            pltpu.VMEM((n_deg, LANES), F32),
            pltpu.VMEM((n_deg, n_h), BF16),
            pltpu.VMEM((own, n_lat, n_rad, LANES), BF16),
            pltpu.VMEM((own, n_lat, n_rad, LANES), BF16),
            pltpu.VMEM((own, n_lat * n_rad, LANES), F32),
            pltpu.VMEM((own, PIECES, n_rad, n_lat // PIECES, LANES), BF16),
            pltpu.VMEM((own, PIECES, n_rad, n_lat // PIECES, LANES), BF16),
            pltpu.VMEM((own, n_rad, n_q, full), BF16),
            pltpu.VMEM((own, PIECES, full, c * n_lat // PIECES), BF16),
            pltpu.VMEM((own, PIECES, n_rad, n_q // PIECES, c * n_lat), BF16),
            dma((3,)), dma((n_l,)), dma, dma, dma,
            dma, dma, dma((own,)), dma((own,)),
            dma((own, PIECES)), dma((own, PIECES)), dma((own, PIECES)), dma((own, PIECES)),
        ],
        compiler_params=pltpu.CompilerParams(
            collective_id=0, has_side_effects=True, vmem_limit_bytes=56 << 20
        ),
    )(
        order_of_slot.reshape(1, n_lat),
        degree_of_slot.reshape(n_deg // block, block),
        degree_count.reshape(1, n_lat),
        rows,
        legendre.reshape(n_deg, n_h),
        inverse,
    )
    return pl.pallas_call(
        widen,
        grid=(own,),
        out_shape=jax.ShapeDtypeStruct((n_rad, own, n_q, c, n_lat), F32),
        in_specs=[
            pl.BlockSpec(
                (1, PIECES, n_rad, n_q // PIECES, c * n_lat), lambda i: (i, 0, 0, 0, 0)
            )
        ],
        out_specs=pl.BlockSpec((n_rad, 1, n_q, c, n_lat), lambda i: (0, i, 0, 0, 0)),
    )(solved).reshape(n_t, n_q, c, n_lat)


def solution(mesh):
    in_specs = (
        P(None, None, "rad", None, None, "lat"),
        P("lat", None, None),
        P("lat", "rad", None),
        P(),
        P(),
        P(),
    )
    out_specs = P("lat", "rad", None, None)
    body = functools.partial(on_device, mesh.shape["lat"], mesh.shape["rad"])
    return jax.shard_map(
        body, mesh=mesh, in_specs=in_specs, out_specs=out_specs, check_vma=False
    )
```

```python
import functools

import jax
import jax.numpy as jnp
from jax import lax
from jax.experimental import pallas as pl
from jax.experimental.pallas import tpu as pltpu
from jax.sharding import PartitionSpec as P

BF16 = jnp.bfloat16
F32 = jnp.float32
MESH = pl.DeviceIdType.MESH
LANES = 128
PIECES = 2


def iota(shape, dim):
    return lax.broadcasted_iota(jnp.int32, shape, dim)


def column(row):
    return jnp.transpose(jnp.broadcast_to(row, (LANES, row.shape[1])))


def dot_nt(a, b):
    return lax.dot_general(a, b, (((1,), (1,)), ((), ())), preferred_element_type=F32)


def farthest_first(k, n):
    if isinstance(k, int):
        return n // 2 + (-((k + 1) // 2) if k % 2 else k // 2)
    return n // 2 + lax.select(lax.rem(k, 2) == 0, k // 2, -((k + 1) // 2))


def kernel(
    dims,
    order_hbm, degree_hbm, count_hbm, rows_hbm, table_hbm, inverse_hbm,
    recv_o,
    order_ref, degree_ref, count_ref, rows, table, north, south, send_folds, recv_folds,
    natural_degree, pick, column_degree, table_live, send_c, recv_c, wide,
    bring_c, got_c, matrices, right_side, send_o,
    small_sem, rows_sem, table_sem, send0, recv0, send1, recv1, send2, recv2, send3, recv3, send4, recv4,
):
    n_lat, n_rad, n_l, n_deg, n_t = dims
    own = n_t // n_rad
    n_q, full = matrices.shape[2], matrices.shape[3]
    radii = full // 2 // n_rad
    me = lax.axis_index("lat")
    y = lax.axis_index("rad")
    group, planes = 8, n_lat // 8
    z, x, core = me // group, lax.rem(me, group) // 2, lax.rem(me, 2)
    places = [
        lax.rem(x + d, 4) * 2 + lax.rem(core + 1 + i, 2) for d in (2, 1, 3, 0) for i in range(2)
    ]

    def ring_of_planes(k):
        return lax.rem(z + farthest_first(k, planes), planes)

    def rad_peer(k):
        return lax.rem(y + farthest_first(k, n_rad), n_rad)

    smalls = [
        pltpu.make_async_copy(src, dst, small_sem.at[i])
        for i, (src, dst) in enumerate(
            ((order_hbm, order_ref), (degree_hbm, degree_ref), (count_hbm, count_ref))
        )
    ]

    def load_rows(l):
        return pltpu.make_async_copy(rows_hbm.at[:, l], rows.at[l], rows_sem.at[l])

    smalls[0].start()
    for l in range(n_l):
        load_rows(l).start()
    smalls[1].start()
    smalls[2].start()
    load_table = pltpu.make_async_copy(table_hbm, table, table_sem)
    load_table.start()

    barrier = pltpu.get_barrier_semaphore()

    def greet_lat(k, carry):
        plane = ring_of_planes(k)
        for place in places:
            pl.semaphore_signal(
                barrier, inc=1, device_id={"lat": plane * group + place}, device_id_type=MESH
            )
        return carry

    def greet_rad(k, carry):
        pl.semaphore_signal(
            barrier, inc=1, device_id={"rad": lax.rem(y + k, n_rad)}, device_id_type=MESH
        )
        return carry

    lax.fori_loop(0, planes - 1, greet_lat, 0)
    for place in places[:-1]:
        pl.semaphore_signal(
            barrier, inc=1, device_id={"lat": z * group + place}, device_id_type=MESH
        )
    lax.fori_loop(1, n_rad, greet_rad, 0)

    smalls[0].wait()
    order = order_ref[...].astype(F32)
    order_column = column(order)[:, :n_lat]
    order_pick = jnp.where(
        order_column == iota((n_lat, n_lat), 1).astype(F32), 1.0, 0.0
    ).astype(BF16)
    load_rows(0).wait()
    for l in range(1, n_l):
        load_rows(l).wait()
    for l in range(n_l):
        picked = dot_nt(order_pick, rows.at[l].reshape(2 * LANES, n_lat)[...])
        north[pl.ds(l, n_lat, stride=n_l), :] = picked[:, :LANES]
        south[pl.ds(l, n_lat, stride=n_l), :] = picked[:, LANES:]

    source, target = iota((2 * LANES, 2 * LANES), 0), iota((2 * LANES, 2 * LANES), 1)
    fold = jnp.where(
        source // 2 == target % LANES,
        jnp.where((source % 2 == 1) & (target >= LANES), -1.0, 1.0),
        0.0,
    ).astype(BF16)

    def fold_plane(k, carry):
        at = pl.ds(pl.multiple_of(k * (2 * group * n_l), 16), 2 * group * n_l)
        both = jnp.concatenate([north[at, :], south[at, :]], axis=1).astype(BF16)
        folded = jnp.dot(both, fold, preferred_element_type=F32).astype(BF16)
        for p in range(2):
            send_folds.at[p].reshape(n_lat * n_l, LANES)[at, :] = folded[
                :, p * LANES:(p + 1) * LANES
            ]
        return carry

    lax.fori_loop(0, planes // 2, fold_plane, 0)

    pl.semaphore_wait(barrier, n_lat + n_rad - 2)

    def send_folded(peer):
        pltpu.make_async_remote_copy(
            src_ref=send_folds.at[:, peer], dst_ref=recv_folds.at[:, me],
            send_sem=send1, recv_sem=recv1,
            device_id={"lat": peer}, device_id_type=MESH,
        ).start()

    for k in range(planes - 1):
        plane = ring_of_planes(k)
        for place in places:
            send_folded(plane * group + place)
    for place in places[:-1]:
        send_folded(z * group + place)
    pltpu.make_async_copy(send_folds.at[:, me], recv_folds.at[:, me], recv1).start()

    def send_matrices(k, carry):
        peer = rad_peer(k)
        pltpu.make_async_remote_copy(
            src_ref=inverse_hbm.at[pl.ds(peer * own, own)], dst_ref=matrices.at[:, y],
            send_sem=send0, recv_sem=recv0,
            device_id={"rad": peer}, device_id_type=MESH,
        ).start()
        return carry

    lax.fori_loop(0, n_rad - 1, send_matrices, 0)
    pltpu.make_async_copy(inverse_hbm.at[pl.ds(y * own, own)], matrices.at[:, y], recv0).start()

    smalls[1].wait()
    smalls[2].wait()
    mine = jnp.sum(jnp.where(iota((1, n_lat), 1) == me, order, 0.0), axis=1, keepdims=True)
    count = jnp.sum(
        jnp.where(iota((1, n_lat), 1).astype(F32) == mine, count_ref[...].astype(F32), 0.0),
        axis=1, keepdims=True,
    )
    first = n_deg - count
    blocks, block = degree_ref.shape

    def to_column(b, carry):
        at = pl.ds(pl.multiple_of(b * block, block), block)
        natural_degree[at, :] = column(degree_ref[pl.ds(b, 1), :].astype(F32))
        return carry

    lax.fori_loop(0, blocks, to_column, 0)
    step = n_deg // own // blocks

    for h in range(own):
        def pick_rows(b, carry):
            held = natural_degree[pl.ds(b * (step * own) + h, step, stride=own), :]
            at = pl.ds(pl.multiple_of(b * step + h * (n_deg // own), step), step)
            column_degree[at, :] = held
            for j in range(blocks):
                lane = (iota((step, block), 1) + j * block).astype(F32)
                cell = held[:, :block]
                pick[at, j * block:(j + 1) * block] = jnp.where(
                    (cell == lane) & (cell >= first), 1.0, 0.0
                ).astype(BF16)
            return carry

        lax.fori_loop(0, blocks, pick_rows, 0)

    load_table.wait()
    rows_at_once = min(256, n_deg // own)

    def order_rows(b, carry):
        at = pl.ds(pl.multiple_of(b * rows_at_once, rows_at_once), rows_at_once)
        table_live[at, :] = jnp.dot(
            pick[at, :], table[...], preferred_element_type=F32
        ).astype(BF16)
        return carry

    lax.fori_loop(0, n_deg // rows_at_once, order_rows, 0)

    pltpu.make_async_copy(recv_folds, recv_folds, recv1).wait()

    parts = n_deg // own // rows_at_once

    reach = planes // parts

    for h in range(own):
        def send(peer):
            pltpu.make_async_remote_copy(
                src_ref=send_c.at[h, peer], dst_ref=recv_c.at[h, me],
                send_sem=send2.at[h], recv_sem=recv2.at[h],
                device_id={"lat": peer}, device_id_type=MESH,
            ).start()

        def analyse_and_send(k, carry):
            part = lax.rem(z // reach + 1 + k, parts)
            begin = pl.multiple_of(part * rows_at_once, rows_at_once)
            at = pl.ds(begin + h * (n_deg // own), rows_at_once)
            both = jnp.concatenate(
                [recv_folds.at[p].reshape(n_lat * n_l, LANES)[...] for p in range(2)], axis=1
            )
            product = jnp.dot(table_live[at, :], both, preferred_element_type=F32)
            parity = (column_degree[at, :] - first).astype(jnp.int32) & 1
            send_c.at[h].reshape(n_lat * n_rad, LANES)[pl.ds(begin, rows_at_once), :] = jnp.where(
                parity == 0, product[:, :LANES], product[:, LANES:]
            ).astype(BF16)

            for j in range(reach):
                plane = part * reach + lax.rem(z + 1 + j, reach)
                for place in places[:-1]:
                    send(plane * group + place)
                last = plane * group + places[-1]
                if j < reach - 1:
                    send(last)
                else:
                    pl.when(last != me)(functools.partial(send, last))
            return carry

        lax.fori_loop(0, parts, analyse_and_send, 0)
        pltpu.make_async_copy(send_c.at[h, me], recv_c.at[h, me], recv2.at[h]).start()

    some = n_lat // PIECES
    for h in range(own):
        pltpu.make_async_copy(recv_c.at[h], recv_c.at[h], recv2.at[h]).wait()
        wide[h] = recv_c.at[h].reshape(n_lat * n_rad, LANES)[...].astype(F32)
        for p in range(PIECES):
            def bring(k, carry):
                peer = rad_peer(k)
                bring_c[h, p, peer] = wide[
                    h, pl.ds(p * some * n_rad + peer, some, stride=n_rad), :
                ].astype(BF16)
                pltpu.make_async_remote_copy(
                    src_ref=bring_c.at[h, p, peer], dst_ref=got_c.at[h, p, y],
                    send_sem=send3.at[h, p], recv_sem=recv3.at[h, p],
                    device_id={"rad": peer}, device_id_type=MESH,
                ).start()
                return carry

            lax.fori_loop(0, n_rad - 1, bring, 0)
            got_c[h, p, y] = wide[
                h, pl.ds(p * some * n_rad + y, some, stride=n_rad), :
            ].astype(BF16)

    pltpu.make_async_copy(matrices, matrices, recv0).wait()
    others = pl.ds(0, n_rad - 1)
    slab = n_q // PIECES
    lanes_of = iota((radii, LANES), 1)
    second_part = lax.rem(lanes_of // some, 2) == 1
    second_half = iota((slab, LANES), 1) >= LANES // PIECES
    for h in range(own):
        for p in range(PIECES):
            pltpu.make_async_copy(
                got_c.at[h, p, others], got_c.at[h, p, others], recv3.at[h, p]
            ).wait()
            for o in range(n_rad):
                block = got_c[h, p, o].astype(F32)
                turned = jnp.transpose(jnp.concatenate([block] * (2 * PIECES), axis=0))
                for f in range(2):
                    at = 2 * f * radii
                    begin = f * (full // 2) + o * radii
                    right_side[h, p, begin:begin + radii, :] = jnp.where(
                        second_part,
                        turned[at + radii:at + 2 * radii, :],
                        turned[at:at + radii, :],
                    ).astype(BF16)
            solved = jnp.dot(
                matrices.at[h].reshape(full, full)[...], right_side[h, p],
                preferred_element_type=F32,
            )
            for o in range(n_rad):
                send_o[h, p, o] = jnp.where(
                    second_half,
                    solved[o * n_q + slab:o * n_q + 2 * slab, :],
                    solved[o * n_q:o * n_q + slab, :],
                ).astype(BF16)

            def give(k, carry):
                peer = rad_peer(k)
                pltpu.make_async_remote_copy(
                    src_ref=send_o.at[h, p, peer], dst_ref=recv_o.at[h, p, y],
                    send_sem=send4.at[h, p], recv_sem=recv4.at[h, p],
                    device_id={"rad": peer}, device_id_type=MESH,
                ).start()
                return carry

            lax.fori_loop(0, n_rad - 1, give, 0)
            pltpu.make_async_copy(
                send_o.at[h, p, y], recv_o.at[h, p, y], recv4.at[h, p]
            ).start()

    for h in range(own):
        for p in range(PIECES):
            pltpu.make_async_copy(recv_o.at[h, p], recv_o.at[h, p], recv4.at[h, p]).wait()

    left = inverse_hbm.at[pl.ds(0, (n_rad - 1) * own)]
    pltpu.make_async_copy(left, left, send0).wait()
    most = pl.ds(0, n_lat - 1)
    pltpu.make_async_copy(send_folds.at[:, most], send_folds.at[:, most], send1).wait()
    for h in range(own):
        pltpu.make_async_copy(send_c.at[h, most], send_c.at[h, most], send2.at[h]).wait()
        for p in range(PIECES):
            sent = bring_c.at[h, p, others]
            pltpu.make_async_copy(sent, sent, send3.at[h, p]).wait()
            sent = send_o.at[h, p, others]
            pltpu.make_async_copy(sent, sent, send4.at[h, p]).wait()


def widen(solved_ref, out_ref):
    n_rad, slab = solved_ref.shape[2:4]
    n_q, n_c, n_lat = out_ref.shape[2:]
    some = n_lat // PIECES
    for o in range(n_rad):
        flat = out_ref.at[o, 0].reshape(n_q * n_c, n_lat)
        block = [solved_ref[0, p, o].astype(F32) for p in range(PIECES)]
        for i in range(PIECES):
            for c in range(n_c):
                begin = (i * n_c + c) * some
                flat[pl.ds(i * slab * n_c + c, slab, stride=n_c), :] = jnp.concatenate(
                    [b[:, begin:begin + some] for b in block], axis=1
                )


def on_device(n_lat, n_rad, fourier, legendre, inverse, order_of_slot, degree_of_slot, degree_count):
    f, c, r, h, m, n_l = fourier.shape
    n_deg, n_h = legendre.shape[1:]
    n_t, n_q, full = inverse.shape
    own = n_t // n_rad
    rows = jnp.transpose(fourier, (0, 1, 2, 5, 3, 4)).reshape(f * c * r, n_l, h, m)
    block = min(LANES, n_deg)
    any_space = pl.BlockSpec(memory_space=pl.ANY)
    dma = pltpu.SemaphoreType.DMA
    pairs = (2, n_lat, n_l // 2, 2, LANES)
    solved = pl.pallas_call(
        functools.partial(kernel, (n_lat, n_rad, n_l, n_deg, n_t)),
        out_shape=jax.ShapeDtypeStruct((own, PIECES, n_rad, n_q // PIECES, c * n_lat), BF16),
        in_specs=[any_space] * 6,
        out_specs=any_space,
        scratch_shapes=[
            pltpu.VMEM((1, n_lat), jnp.int32),
            pltpu.VMEM((n_deg // block, block), jnp.int32),
            pltpu.VMEM((1, n_lat), jnp.int32),
            pltpu.VMEM((n_l, f * c * r, h, m), BF16),
            pltpu.VMEM((n_deg, n_h), BF16),
            pltpu.VMEM((n_lat * n_l, LANES), F32),
            pltpu.VMEM((n_lat * n_l, LANES), F32),
            pltpu.VMEM(pairs, BF16),
            pltpu.VMEM(pairs, BF16),
            pltpu.VMEM((n_deg, LANES), F32),
            pltpu.VMEM((n_deg, n_deg), BF16),
            pltpu.VMEM((n_deg, LANES), F32),
            pltpu.VMEM((n_deg, n_h), BF16),
            pltpu.VMEM((own, n_lat, n_rad, LANES), BF16),
            pltpu.VMEM((own, n_lat, n_rad, LANES), BF16),
            pltpu.VMEM((own, n_lat * n_rad, LANES), F32),
            pltpu.VMEM((own, PIECES, n_rad, n_lat // PIECES, LANES), BF16),
            pltpu.VMEM((own, PIECES, n_rad, n_lat // PIECES, LANES), BF16),
            pltpu.VMEM((own, n_rad, n_q, full), BF16),
            pltpu.VMEM((own, PIECES, full, c * n_lat), BF16),
            pltpu.VMEM((own, PIECES, n_rad, n_q // PIECES, c * n_lat), BF16),
            dma((3,)), dma((n_l,)), dma, dma, dma,
            dma, dma, dma((own,)), dma((own,)),
            dma((own, PIECES)), dma((own, PIECES)), dma((own, PIECES)), dma((own, PIECES)),
        ],
        compiler_params=pltpu.CompilerParams(
            collective_id=0, has_side_effects=True, vmem_limit_bytes=56 << 20
        ),
    )(
        order_of_slot.reshape(1, n_lat),
        degree_of_slot.reshape(n_deg // block, block),
        degree_count.reshape(1, n_lat),
        rows,
        legendre.reshape(n_deg, n_h),
        inverse,
    )
    return pl.pallas_call(
        widen,
        grid=(own,),
        out_shape=jax.ShapeDtypeStruct((n_rad, own, n_q, c, n_lat), F32),
        in_specs=[
            pl.BlockSpec(
                (1, PIECES, n_rad, n_q // PIECES, c * n_lat), lambda i: (i, 0, 0, 0, 0)
            )
        ],
        out_specs=pl.BlockSpec((n_rad, 1, n_q, c, n_lat), lambda i: (0, i, 0, 0, 0)),
    )(solved).reshape(n_t, n_q, c, n_lat)


def solution(mesh):
    in_specs = (
        P(None, None, "rad", None, None, "lat"),
        P("lat", None, None),
        P("lat", "rad", None),
        P(),
        P(),
        P(),
    )
    out_specs = P("lat", "rad", None, None)
    body = functools.partial(on_device, mesh.shape["lat"], mesh.shape["rad"])
    return jax.shard_map(
        body, mesh=mesh, in_specs=in_specs, out_specs=out_specs, check_vma=False
    )
```

```python
import functools

import jax
import jax.numpy as jnp
from jax import lax
from jax.experimental import pallas as pl
from jax.experimental.pallas import tpu as pltpu
from jax.sharding import PartitionSpec as P

BF16 = jnp.bfloat16
F32 = jnp.float32
MESH = pl.DeviceIdType.MESH
LANES = 128
PIECES = 2


def iota(shape, dim):
    return lax.broadcasted_iota(jnp.int32, shape, dim)


def column(row):
    return jnp.transpose(jnp.broadcast_to(row, (LANES, row.shape[1])))


def dot_nt(a, b):
    return lax.dot_general(a, b, (((1,), (1,)), ((), ())), preferred_element_type=F32)


def farthest_first(k, n):
    if isinstance(k, int):
        return n // 2 + (-((k + 1) // 2) if k % 2 else k // 2)
    return n // 2 + lax.select(lax.rem(k, 2) == 0, k // 2, -((k + 1) // 2))


def kernel(
    dims,
    small_hbm, rows_hbm, table_hbm, inverse_hbm,
    recv_o,
    small, rows, table, north, south, send_folds, recv_folds,
    natural_degree, pick, column_degree, table_live, send_c, recv_c, wide,
    bring_c, got_c, matrices, right_side, send_o,
    small_sem, rows_sem, table_sem, send0, recv0, send1, recv1, send2, recv2, send3, recv3, send4, recv4,
):
    n_lat, n_rad, n_l, n_deg, n_t = dims
    own = n_t // n_rad
    n_q, full = matrices.shape[2], matrices.shape[3]
    radii = full // 2 // n_rad
    me = lax.axis_index("lat")
    y = lax.axis_index("rad")
    group, planes = 8, n_lat // 8
    z, x, core = me // group, lax.rem(me, group) // 2, lax.rem(me, 2)
    places = [
        lax.rem(x + d, 4) * 2 + lax.rem(core + 1 + i, 2) for d in (2, 1, 3, 0) for i in range(2)
    ]

    def ring_of_planes(k):
        return lax.rem(z + farthest_first(k, planes), planes)

    def rad_peer(k):
        return lax.rem(y + farthest_first(k, n_rad), n_rad)

    load_small = pltpu.make_async_copy(small_hbm, small, small_sem)

    def load_rows(l):
        return pltpu.make_async_copy(rows_hbm.at[:, l], rows.at[l], rows_sem.at[l])

    load_small.start()
    for l in range(n_l):
        load_rows(l).start()
    load_table = pltpu.make_async_copy(table_hbm, table, table_sem)
    load_table.start()

    barrier = pltpu.get_barrier_semaphore()

    def greet_lat(k, carry):
        plane = ring_of_planes(k)
        for place in places:
            pl.semaphore_signal(
                barrier, inc=1, device_id={"lat": plane * group + place}, device_id_type=MESH
            )
        return carry

    def greet_rad(k, carry):
        pl.semaphore_signal(
            barrier, inc=1, device_id={"rad": lax.rem(y + k, n_rad)}, device_id_type=MESH
        )
        return carry

    lax.fori_loop(0, planes - 1, greet_lat, 0)
    for place in places[:-1]:
        pl.semaphore_signal(
            barrier, inc=1, device_id={"lat": z * group + place}, device_id_type=MESH
        )
    lax.fori_loop(1, n_rad, greet_rad, 0)

    load_small.wait()
    order = small[0:1, :n_lat].astype(F32)
    order_column = column(order)[:, :n_lat]
    order_pick = jnp.where(
        order_column == iota((n_lat, n_lat), 1).astype(F32), 1.0, 0.0
    ).astype(BF16)
    load_rows(0).wait()
    for l in range(1, n_l):
        load_rows(l).wait()
    for l in range(n_l):
        picked = dot_nt(order_pick, rows.at[l].reshape(2 * LANES, n_lat)[...])
        north[pl.ds(l, n_lat, stride=n_l), :] = picked[:, :LANES]
        south[pl.ds(l, n_lat, stride=n_l), :] = picked[:, LANES:]

    source, target = iota((2 * LANES, 2 * LANES), 0), iota((2 * LANES, 2 * LANES), 1)
    fold = jnp.where(
        source // 2 == target % LANES,
        jnp.where((source % 2 == 1) & (target >= LANES), -1.0, 1.0),
        0.0,
    ).astype(BF16)

    def fold_plane(k, carry):
        at = pl.ds(pl.multiple_of(k * (2 * group * n_l), 16), 2 * group * n_l)
        both = jnp.concatenate([north[at, :], south[at, :]], axis=1).astype(BF16)
        folded = jnp.dot(both, fold, preferred_element_type=F32).astype(BF16)
        for p in range(2):
            send_folds.at[p].reshape(n_lat * n_l, LANES)[at, :] = folded[
                :, p * LANES:(p + 1) * LANES
            ]
        return carry

    lax.fori_loop(0, planes // 2, fold_plane, 0)

    pl.semaphore_wait(barrier, n_lat + n_rad - 2)

    def send_folded(peer):
        pltpu.make_async_remote_copy(
            src_ref=send_folds.at[:, peer], dst_ref=recv_folds.at[:, me],
            send_sem=send1, recv_sem=recv1,
            device_id={"lat": peer}, device_id_type=MESH,
        ).start()

    for k in range(planes - 1):
        plane = ring_of_planes(k)
        for place in places:
            send_folded(plane * group + place)
    for place in places[:-1]:
        send_folded(z * group + place)
    pltpu.make_async_copy(send_folds.at[:, me], recv_folds.at[:, me], recv1).start()

    def send_matrices(k, carry):
        peer = rad_peer(k)
        pltpu.make_async_remote_copy(
            src_ref=inverse_hbm.at[pl.ds(peer * own, own)], dst_ref=matrices.at[:, y],
            send_sem=send0, recv_sem=recv0,
            device_id={"rad": peer}, device_id_type=MESH,
        ).start()
        return carry

    lax.fori_loop(0, n_rad - 1, send_matrices, 0)
    pltpu.make_async_copy(inverse_hbm.at[pl.ds(y * own, own)], matrices.at[:, y], recv0).start()

    mine = jnp.sum(jnp.where(iota((1, n_lat), 1) == me, order, 0.0), axis=1, keepdims=True)
    count = jnp.sum(
        jnp.where(iota((1, n_lat), 1).astype(F32) == mine, small[0:1, n_lat:2 * n_lat].astype(F32), 0.0),
        axis=1, keepdims=True,
    )
    first = n_deg - count
    blocks, block = small.shape[0] - 1, small.shape[1]

    def to_column(b, carry):
        at = pl.ds(pl.multiple_of(b * block, block), block)
        natural_degree[at, :] = column(small[pl.ds(b + 1, 1), :].astype(F32))
        return carry

    lax.fori_loop(0, blocks, to_column, 0)
    step = n_deg // own // blocks

    for h in range(own):
        def pick_rows(b, carry):
            held = natural_degree[pl.ds(b * (step * own) + h, step, stride=own), :]
            at = pl.ds(pl.multiple_of(b * step + h * (n_deg // own), step), step)
            column_degree[at, :] = held
            for j in range(blocks):
                lane = (iota((step, block), 1) + j * block).astype(F32)
                cell = held[:, :block]
                pick[at, j * block:(j + 1) * block] = jnp.where(
                    (cell == lane) & (cell >= first), 1.0, 0.0
                ).astype(BF16)
            return carry

        lax.fori_loop(0, blocks, pick_rows, 0)

    load_table.wait()
    rows_at_once = min(256, n_deg // own)

    def order_rows(b, carry):
        at = pl.ds(pl.multiple_of(b * rows_at_once, rows_at_once), rows_at_once)
        table_live[at, :] = jnp.dot(
            pick[at, :], table[...], preferred_element_type=F32
        ).astype(BF16)
        return carry

    lax.fori_loop(0, n_deg // rows_at_once, order_rows, 0)

    pltpu.make_async_copy(recv_folds, recv_folds, recv1).wait()

    parts = n_deg // own // rows_at_once

    reach = planes // parts

    for h in range(own):
        def send(peer):
            pltpu.make_async_remote_copy(
                src_ref=send_c.at[h, peer], dst_ref=recv_c.at[h, me],
                send_sem=send2.at[h], recv_sem=recv2.at[h],
                device_id={"lat": peer}, device_id_type=MESH,
            ).start()

        def analyse_and_send(k, carry):
            part = lax.rem(z // reach + 1 + k, parts)
            begin = pl.multiple_of(part * rows_at_once, rows_at_once)
            at = pl.ds(begin + h * (n_deg // own), rows_at_once)
            both = jnp.concatenate(
                [recv_folds.at[p].reshape(n_lat * n_l, LANES)[...] for p in range(2)], axis=1
            )
            product = jnp.dot(table_live[at, :], both, preferred_element_type=F32)
            parity = (column_degree[at, :] - first).astype(jnp.int32) & 1
            send_c.at[h].reshape(n_lat * n_rad, LANES)[pl.ds(begin, rows_at_once), :] = jnp.where(
                parity == 0, product[:, :LANES], product[:, LANES:]
            ).astype(BF16)

            for j in range(reach):
                plane = part * reach + lax.rem(z + 1 + j, reach)
                for place in places[:-1]:
                    send(plane * group + place)
                last = plane * group + places[-1]
                if j < reach - 1:
                    send(last)
                else:
                    pl.when(last != me)(functools.partial(send, last))
            return carry

        lax.fori_loop(0, parts, analyse_and_send, 0)
        pltpu.make_async_copy(send_c.at[h, me], recv_c.at[h, me], recv2.at[h]).start()

    some = n_lat // PIECES
    for h in range(own):
        pltpu.make_async_copy(recv_c.at[h], recv_c.at[h], recv2.at[h]).wait()
        wide[h] = recv_c.at[h].reshape(n_lat * n_rad, LANES)[...].astype(F32)
        for p in range(PIECES):
            def bring(k, carry):
                peer = rad_peer(k)
                bring_c[h, p, peer] = wide[
                    h, pl.ds(p * some * n_rad + peer, some, stride=n_rad), :
                ].astype(BF16)
                pltpu.make_async_remote_copy(
                    src_ref=bring_c.at[h, p, peer], dst_ref=got_c.at[h, p, y],
                    send_sem=send3.at[h, p], recv_sem=recv3.at[h, p],
                    device_id={"rad": peer}, device_id_type=MESH,
                ).start()
                return carry

            lax.fori_loop(0, n_rad - 1, bring, 0)
            got_c[h, p, y] = wide[
                h, pl.ds(p * some * n_rad + y, some, stride=n_rad), :
            ].astype(BF16)

    pltpu.make_async_copy(matrices, matrices, recv0).wait()
    others = pl.ds(0, n_rad - 1)
    slab = n_q // PIECES
    lanes_of = iota((radii, LANES), 1)
    second_part = lax.rem(lanes_of // some, 2) == 1
    second_half = iota((slab, LANES), 1) >= LANES // PIECES
    for h in range(own):
        for p in range(PIECES):
            pltpu.make_async_copy(
                got_c.at[h, p, others], got_c.at[h, p, others], recv3.at[h, p]
            ).wait()
            for o in range(n_rad):
                block = got_c[h, p, o].astype(F32)
                turned = jnp.transpose(jnp.concatenate([block] * (2 * PIECES), axis=0))
                for f in range(2):
                    at = 2 * f * radii
                    begin = f * (full // 2) + o * radii
                    right_side[h, p, begin:begin + radii, :] = jnp.where(
                        second_part,
                        turned[at + radii:at + 2 * radii, :],
                        turned[at:at + radii, :],
                    ).astype(BF16)
            solved = jnp.dot(
                matrices.at[h].reshape(full, full)[...], right_side[h, p],
                preferred_element_type=F32,
            )
            for o in range(n_rad):
                send_o[h, p, o] = jnp.where(
                    second_half,
                    solved[o * n_q + slab:o * n_q + 2 * slab, :],
                    solved[o * n_q:o * n_q + slab, :],
                ).astype(BF16)

            def give(k, carry):
                peer = rad_peer(k)
                pltpu.make_async_remote_copy(
                    src_ref=send_o.at[h, p, peer], dst_ref=recv_o.at[h, p, y],
                    send_sem=send4.at[h, p], recv_sem=recv4.at[h, p],
                    device_id={"rad": peer}, device_id_type=MESH,
                ).start()
                return carry

            lax.fori_loop(0, n_rad - 1, give, 0)
            pltpu.make_async_copy(
                send_o.at[h, p, y], recv_o.at[h, p, y], recv4.at[h, p]
            ).start()

    for h in range(own):
        for p in range(PIECES):
            pltpu.make_async_copy(recv_o.at[h, p], recv_o.at[h, p], recv4.at[h, p]).wait()

    left = inverse_hbm.at[pl.ds(0, (n_rad - 1) * own)]
    pltpu.make_async_copy(left, left, send0).wait()
    most = pl.ds(0, n_lat - 1)
    pltpu.make_async_copy(send_folds.at[:, most], send_folds.at[:, most], send1).wait()
    for h in range(own):
        pltpu.make_async_copy(send_c.at[h, most], send_c.at[h, most], send2.at[h]).wait()
        for p in range(PIECES):
            sent = bring_c.at[h, p, others]
            pltpu.make_async_copy(sent, sent, send3.at[h, p]).wait()
            sent = send_o.at[h, p, others]
            pltpu.make_async_copy(sent, sent, send4.at[h, p]).wait()


def widen(solved_ref, out_ref):
    n_rad, slab = solved_ref.shape[2:4]
    n_q, n_c, n_lat = out_ref.shape[2:]
    some = n_lat // PIECES
    for o in range(n_rad):
        flat = out_ref.at[o, 0].reshape(n_q * n_c, n_lat)
        block = [solved_ref[0, p, o].astype(F32) for p in range(PIECES)]
        for i in range(PIECES):
            for c in range(n_c):
                begin = (i * n_c + c) * some
                flat[pl.ds(i * slab * n_c + c, slab, stride=n_c), :] = jnp.concatenate(
                    [b[:, begin:begin + some] for b in block], axis=1
                )


def on_device(n_lat, n_rad, fourier, legendre, inverse, order_of_slot, degree_of_slot, degree_count):
    f, c, r, h, m, n_l = fourier.shape
    n_deg, n_h = legendre.shape[1:]
    n_t, n_q, full = inverse.shape
    own = n_t // n_rad
    rows = jnp.transpose(fourier, (0, 1, 2, 5, 3, 4)).reshape(f * c * r, n_l, h, m)
    block = min(LANES, n_deg)
    any_space = pl.BlockSpec(memory_space=pl.ANY)
    dma = pltpu.SemaphoreType.DMA
    pairs = (2, n_lat, n_l // 2, 2, LANES)
    solved = pl.pallas_call(
        functools.partial(kernel, (n_lat, n_rad, n_l, n_deg, n_t)),
        out_shape=jax.ShapeDtypeStruct((own, PIECES, n_rad, n_q // PIECES, c * n_lat), BF16),
        in_specs=[any_space] * 4,
        out_specs=any_space,
        scratch_shapes=[
            pltpu.VMEM((n_deg // block + 1, block), jnp.int32),
            pltpu.VMEM((n_l, f * c * r, h, m), BF16),
            pltpu.VMEM((n_deg, n_h), BF16),
            pltpu.VMEM((n_lat * n_l, LANES), F32),
            pltpu.VMEM((n_lat * n_l, LANES), F32),
            pltpu.VMEM(pairs, BF16),
            pltpu.VMEM(pairs, BF16),
            pltpu.VMEM((n_deg, LANES), F32),
            pltpu.VMEM((n_deg, n_deg), BF16),
            pltpu.VMEM((n_deg, LANES), F32),
            pltpu.VMEM((n_deg, n_h), BF16),
            pltpu.VMEM((own, n_lat, n_rad, LANES), BF16),
            pltpu.VMEM((own, n_lat, n_rad, LANES), BF16),
            pltpu.VMEM((own, n_lat * n_rad, LANES), F32),
            pltpu.VMEM((own, PIECES, n_rad, n_lat // PIECES, LANES), BF16),
            pltpu.VMEM((own, PIECES, n_rad, n_lat // PIECES, LANES), BF16),
            pltpu.VMEM((own, n_rad, n_q, full), BF16),
            pltpu.VMEM((own, PIECES, full, c * n_lat), BF16),
            pltpu.VMEM((own, PIECES, n_rad, n_q // PIECES, c * n_lat), BF16),
            dma, dma((n_l,)), dma, dma, dma,
            dma, dma, dma((own,)), dma((own,)),
            dma((own, PIECES)), dma((own, PIECES)), dma((own, PIECES)), dma((own, PIECES)),
        ],
        compiler_params=pltpu.CompilerParams(
            collective_id=0, has_side_effects=True, vmem_limit_bytes=53 << 20
        ),
    )(
        jnp.concatenate([order_of_slot, degree_count, degree_of_slot]).reshape(-1, block),
        rows,
        legendre.reshape(n_deg, n_h),
        inverse,
    )
    return pl.pallas_call(
        widen,
        grid=(own,),
        out_shape=jax.ShapeDtypeStruct((n_rad, own, n_q, c, n_lat), F32),
        in_specs=[
            pl.BlockSpec(
                (1, PIECES, n_rad, n_q // PIECES, c * n_lat), lambda i: (i, 0, 0, 0, 0)
            )
        ],
        out_specs=pl.BlockSpec((n_rad, 1, n_q, c, n_lat), lambda i: (0, i, 0, 0, 0)),
        compiler_params=pltpu.CompilerParams(vmem_limit_bytes=8 << 20),
    )(solved).reshape(n_t, n_q, c, n_lat)


def solution(mesh):
    in_specs = (
        P(None, None, "rad", None, None, "lat"),
        P("lat", None, None),
        P("lat", "rad", None),
        P(),
        P(),
        P(),
    )
    out_specs = P("lat", "rad", None, None)
    body = functools.partial(on_device, mesh.shape["lat"], mesh.shape["rad"])
    return jax.shard_map(
        body, mesh=mesh, in_specs=in_specs, out_specs=out_specs, check_vma=False
    )
```

```python
import functools

import jax
import jax.numpy as jnp
from jax import lax
from jax.experimental import pallas as pl
from jax.experimental.pallas import tpu as pltpu
from jax.sharding import PartitionSpec as P

BF16 = jnp.bfloat16
F32 = jnp.float32
MESH = pl.DeviceIdType.MESH
LANES = 128
PIECES = 2


def iota(shape, dim):
    return lax.broadcasted_iota(jnp.int32, shape, dim)


def column(row):
    return jnp.transpose(jnp.broadcast_to(row, (LANES, row.shape[1])))


def dot_nt(a, b):
    return lax.dot_general(a, b, (((1,), (1,)), ((), ())), preferred_element_type=F32)


def farthest_first(k, n):
    if isinstance(k, int):
        return n // 2 + (-((k + 1) // 2) if k % 2 else k // 2)
    return n // 2 + lax.select(lax.rem(k, 2) == 0, k // 2, -((k + 1) // 2))


def kernel(
    dims,
    small_hbm, rows_hbm, table_hbm, inverse_hbm,
    recv_o,
    small, rows, table, north, south, send_folds, recv_folds,
    natural_degree, pick, column_degree, table_live, send_c, recv_c, wide,
    bring_c, got_c, matrices, right_side, send_o,
    small_sem, rows_sem, table_sem, send0, recv0, send1, recv1, send2, recv2, send3, recv3, send4, recv4,
):
    n_lat, n_rad, n_l, n_deg, n_t = dims
    own = n_t // n_rad
    n_q, full = matrices.shape[2], matrices.shape[3]
    radii = full // 2 // n_rad
    me = lax.axis_index("lat")
    y = lax.axis_index("rad")
    group, planes = 8, n_lat // 8
    z, x, core = me // group, lax.rem(me, group) // 2, lax.rem(me, 2)
    places = [
        lax.rem(x + d, 4) * 2 + lax.rem(core + 1 + i, 2) for d in (2, 1, 3, 0) for i in range(2)
    ]

    def ring_of_planes(k):
        return lax.rem(z + farthest_first(k, planes), planes)

    def rad_peer(k):
        return lax.rem(y + farthest_first(k, n_rad), n_rad)

    load_small = pltpu.make_async_copy(small_hbm, small, small_sem)

    def load_rows(l):
        return pltpu.make_async_copy(rows_hbm.at[:, l], rows.at[l], rows_sem.at[l])

    load_small.start()
    for l in range(n_l):
        load_rows(l).start()
    load_table = pltpu.make_async_copy(table_hbm, table, table_sem)
    load_table.start()

    barrier = pltpu.get_barrier_semaphore()

    def greet_lat(k, carry):
        plane = ring_of_planes(k)
        for place in places:
            pl.semaphore_signal(
                barrier, inc=1, device_id={"lat": plane * group + place}, device_id_type=MESH
            )
        return carry

    def greet_rad(k, carry):
        pl.semaphore_signal(
            barrier, inc=1, device_id={"rad": lax.rem(y + k, n_rad)}, device_id_type=MESH
        )
        return carry

    lax.fori_loop(0, planes - 1, greet_lat, 0)
    for place in places[:-1]:
        pl.semaphore_signal(
            barrier, inc=1, device_id={"lat": z * group + place}, device_id_type=MESH
        )
    lax.fori_loop(1, n_rad, greet_rad, 0)

    load_small.wait()
    order = small[0:1, :n_lat].astype(F32)
    order_column = column(order)[:, :n_lat]
    order_pick = jnp.where(
        order_column == iota((n_lat, n_lat), 1).astype(F32), 1.0, 0.0
    ).astype(BF16)
    load_rows(0).wait()
    for l in range(1, n_l):
        load_rows(l).wait()
    for l in range(n_l):
        picked = dot_nt(order_pick, rows.at[l].reshape(2 * LANES, n_lat)[...])
        north[pl.ds(l, n_lat, stride=n_l), :] = picked[:, :LANES]
        south[pl.ds(l, n_lat, stride=n_l), :] = picked[:, LANES:]

    source, target = iota((2 * LANES, 2 * LANES), 0), iota((2 * LANES, 2 * LANES), 1)
    fold = jnp.where(
        source // 2 == target % LANES,
        jnp.where((source % 2 == 1) & (target >= LANES), -1.0, 1.0),
        0.0,
    ).astype(BF16)

    def fold_plane(k, carry):
        at = pl.ds(pl.multiple_of(k * (2 * group * n_l), 16), 2 * group * n_l)
        both = jnp.concatenate([north[at, :], south[at, :]], axis=1).astype(BF16)
        folded = jnp.dot(both, fold, preferred_element_type=F32).astype(BF16)
        for p in range(2):
            send_folds.at[p].reshape(n_lat * n_l, LANES)[at, :] = folded[
                :, p * LANES:(p + 1) * LANES
            ]
        return carry

    lax.fori_loop(0, planes // 2, fold_plane, 0)

    pl.semaphore_wait(barrier, n_lat + n_rad - 2)

    def send_folded(peer):
        pltpu.make_async_remote_copy(
            src_ref=send_folds.at[:, peer], dst_ref=recv_folds.at[:, me],
            send_sem=send1, recv_sem=recv1,
            device_id={"lat": peer}, device_id_type=MESH,
        ).start()

    for k in range(planes - 1):
        plane = ring_of_planes(k)
        for place in places:
            send_folded(plane * group + place)
    for place in places[:-1]:
        send_folded(z * group + place)
    pltpu.make_async_copy(send_folds.at[:, me], recv_folds.at[:, me], recv1).start()

    def send_matrices(k, carry):
        peer = rad_peer(k)
        pltpu.make_async_remote_copy(
            src_ref=inverse_hbm.at[pl.ds(peer * own, own)], dst_ref=matrices.at[:, y],
            send_sem=send0, recv_sem=recv0,
            device_id={"rad": peer}, device_id_type=MESH,
        ).start()
        return carry

    lax.fori_loop(0, n_rad - 1, send_matrices, 0)
    pltpu.make_async_copy(inverse_hbm.at[pl.ds(y * own, own)], matrices.at[:, y], recv0).start()

    mine = jnp.sum(jnp.where(iota((1, n_lat), 1) == me, order, 0.0), axis=1, keepdims=True)
    count = jnp.sum(
        jnp.where(iota((1, n_lat), 1).astype(F32) == mine, small[0:1, n_lat:2 * n_lat].astype(F32), 0.0),
        axis=1, keepdims=True,
    )
    first = n_deg - count
    blocks, block = small.shape[0] - 1, small.shape[1]

    def to_column(b, carry):
        at = pl.ds(pl.multiple_of(b * block, block), block)
        natural_degree[at, :] = column(small[pl.ds(b + 1, 1), :].astype(F32))
        return carry

    lax.fori_loop(0, blocks, to_column, 0)
    step = n_deg // own // blocks

    for h in range(own):
        def pick_rows(b, carry):
            held = natural_degree[pl.ds(b * (step * own) + h, step, stride=own), :]
            at = pl.ds(pl.multiple_of(b * step + h * (n_deg // own), step), step)
            column_degree[at, :] = held
            for j in range(blocks):
                lane = (iota((step, block), 1) + j * block).astype(F32)
                cell = held[:, :block]
                pick[at, j * block:(j + 1) * block] = jnp.where(
                    (cell == lane) & (cell >= first), 1.0, 0.0
                ).astype(BF16)
            return carry

        lax.fori_loop(0, blocks, pick_rows, 0)

    load_table.wait()
    rows_at_once = min(256, n_deg // own)

    def order_rows(b, carry):
        at = pl.ds(pl.multiple_of(b * rows_at_once, rows_at_once), rows_at_once)
        table_live[at, :] = jnp.dot(
            pick[at, :], table[...], preferred_element_type=F32
        ).astype(BF16)
        return carry

    lax.fori_loop(0, n_deg // rows_at_once, order_rows, 0)

    pltpu.make_async_copy(recv_folds, recv_folds, recv1).wait()

    parts = n_deg // own // rows_at_once

    reach = planes // parts

    for h in range(own):
        def send(peer):
            pltpu.make_async_remote_copy(
                src_ref=send_c.at[h, peer], dst_ref=recv_c.at[h, me],
                send_sem=send2.at[h], recv_sem=recv2.at[h],
                device_id={"lat": peer}, device_id_type=MESH,
            ).start()

        def analyse_and_send(k, carry):
            part = lax.rem(z // reach + 1 + k, parts)
            begin = pl.multiple_of(part * rows_at_once, rows_at_once)
            at = pl.ds(begin + h * (n_deg // own), rows_at_once)
            both = jnp.concatenate(
                [recv_folds.at[p].reshape(n_lat * n_l, LANES)[...] for p in range(2)], axis=1
            )
            product = jnp.dot(table_live[at, :], both, preferred_element_type=F32)
            parity = (column_degree[at, :] - first).astype(jnp.int32) & 1
            send_c.at[h].reshape(n_lat * n_rad, LANES)[pl.ds(begin, rows_at_once), :] = jnp.where(
                parity == 0, product[:, :LANES], product[:, LANES:]
            ).astype(BF16)

            for j in range(reach):
                plane = part * reach + lax.rem(z + 1 + j, reach)
                for place in places[:-1]:
                    send(plane * group + place)
                last = plane * group + places[-1]
                if j < reach - 1:
                    send(last)
                else:
                    pl.when(last != me)(functools.partial(send, last))
            return carry

        lax.fori_loop(0, parts, analyse_and_send, 0)
        pltpu.make_async_copy(send_c.at[h, me], recv_c.at[h, me], recv2.at[h]).start()

    some = n_lat // PIECES
    for h in range(own):
        pltpu.make_async_copy(recv_c.at[h], recv_c.at[h], recv2.at[h]).wait()
        wide[h] = recv_c.at[h].reshape(n_lat * n_rad, LANES)[...].astype(F32)
        for p in range(PIECES):
            def bring(k, carry):
                peer = rad_peer(k)
                bring_c[h, p, peer] = wide[
                    h, pl.ds(p * some * n_rad + peer, some, stride=n_rad), :
                ].astype(BF16)
                pltpu.make_async_remote_copy(
                    src_ref=bring_c.at[h, p, peer], dst_ref=got_c.at[h, p, y],
                    send_sem=send3.at[h, p], recv_sem=recv3.at[h, p],
                    device_id={"rad": peer}, device_id_type=MESH,
                ).start()
                return carry

            lax.fori_loop(0, n_rad - 1, bring, 0)
            got_c[h, p, y] = wide[
                h, pl.ds(p * some * n_rad + y, some, stride=n_rad), :
            ].astype(BF16)

    pltpu.make_async_copy(matrices, matrices, recv0).wait()
    others = pl.ds(0, n_rad - 1)
    slab = n_q // PIECES
    lanes_of = iota((radii, LANES), 1)
    second_part = lax.rem(lanes_of // some, 2) == 1
    second_half = iota((slab, LANES), 1) >= LANES // PIECES
    for h in range(own):
        for p in range(PIECES):
            pltpu.make_async_copy(
                got_c.at[h, p, others], got_c.at[h, p, others], recv3.at[h, p]
            ).wait()
            for o in range(n_rad):
                block = got_c[h, p, o]
                turned = jnp.transpose(jnp.concatenate([block] * (2 * PIECES), axis=0))
                for f in range(2):
                    at = 2 * f * radii
                    begin = f * (full // 2) + o * radii
                    right_side[h, p, begin:begin + radii, :] = jnp.where(
                        second_part,
                        turned[at + radii:at + 2 * radii, :].astype(F32),
                        turned[at:at + radii, :].astype(F32),
                    ).astype(BF16)
            solved = jnp.dot(
                matrices.at[h].reshape(full, full)[...], right_side[h, p],
                preferred_element_type=F32,
            )
            for o in range(n_rad):
                send_o[h, p, o] = jnp.where(
                    second_half,
                    solved[o * n_q + slab:o * n_q + 2 * slab, :],
                    solved[o * n_q:o * n_q + slab, :],
                ).astype(BF16)

            def give(k, carry):
                peer = rad_peer(k)
                pltpu.make_async_remote_copy(
                    src_ref=send_o.at[h, p, peer], dst_ref=recv_o.at[h, p, y],
                    send_sem=send4.at[h, p], recv_sem=recv4.at[h, p],
                    device_id={"rad": peer}, device_id_type=MESH,
                ).start()
                return carry

            lax.fori_loop(0, n_rad - 1, give, 0)
            pltpu.make_async_copy(
                send_o.at[h, p, y], recv_o.at[h, p, y], recv4.at[h, p]
            ).start()

    for h in range(own):
        for p in range(PIECES):
            pltpu.make_async_copy(recv_o.at[h, p], recv_o.at[h, p], recv4.at[h, p]).wait()

    left = inverse_hbm.at[pl.ds(0, (n_rad - 1) * own)]
    pltpu.make_async_copy(left, left, send0).wait()
    most = pl.ds(0, n_lat - 1)
    pltpu.make_async_copy(send_folds.at[:, most], send_folds.at[:, most], send1).wait()
    for h in range(own):
        pltpu.make_async_copy(send_c.at[h, most], send_c.at[h, most], send2.at[h]).wait()
        for p in range(PIECES):
            sent = bring_c.at[h, p, others]
            pltpu.make_async_copy(sent, sent, send3.at[h, p]).wait()
            sent = send_o.at[h, p, others]
            pltpu.make_async_copy(sent, sent, send4.at[h, p]).wait()


def widen(solved_ref, out_ref):
    n_rad, slab = solved_ref.shape[2:4]
    n_q, n_c, n_lat = out_ref.shape[2:]
    some = n_lat // PIECES
    for o in range(n_rad):
        flat = out_ref.at[o, 0].reshape(n_q * n_c, n_lat)
        block = [solved_ref[0, p, o].astype(F32) for p in range(PIECES)]
        for i in range(PIECES):
            for c in range(n_c):
                begin = (i * n_c + c) * some
                flat[pl.ds(i * slab * n_c + c, slab, stride=n_c), :] = jnp.concatenate(
                    [b[:, begin:begin + some] for b in block], axis=1
                )


def on_device(n_lat, n_rad, fourier, legendre, inverse, order_of_slot, degree_of_slot, degree_count):
    f, c, r, h, m, n_l = fourier.shape
    n_deg, n_h = legendre.shape[1:]
    n_t, n_q, full = inverse.shape
    own = n_t // n_rad
    rows = jnp.transpose(fourier, (0, 1, 2, 5, 3, 4)).reshape(f * c * r, n_l, h, m)
    block = min(LANES, n_deg)
    any_space = pl.BlockSpec(memory_space=pl.ANY)
    dma = pltpu.SemaphoreType.DMA
    pairs = (2, n_lat, n_l // 2, 2, LANES)
    solved = pl.pallas_call(
        functools.partial(kernel, (n_lat, n_rad, n_l, n_deg, n_t)),
        out_shape=jax.ShapeDtypeStruct((own, PIECES, n_rad, n_q // PIECES, c * n_lat), BF16),
        in_specs=[any_space] * 4,
        out_specs=any_space,
        scratch_shapes=[
            pltpu.VMEM((n_deg // block + 1, block), jnp.int32),
            pltpu.VMEM((n_l, f * c * r, h, m), BF16),
            pltpu.VMEM((n_deg, n_h), BF16),
            pltpu.VMEM((n_lat * n_l, LANES), F32),
            pltpu.VMEM((n_lat * n_l, LANES), F32),
            pltpu.VMEM(pairs, BF16),
            pltpu.VMEM(pairs, BF16),
            pltpu.VMEM((n_deg, LANES), F32),
            pltpu.VMEM((n_deg, n_deg), BF16),
            pltpu.VMEM((n_deg, LANES), F32),
            pltpu.VMEM((n_deg, n_h), BF16),
            pltpu.VMEM((own, n_lat, n_rad, LANES), BF16),
            pltpu.VMEM((own, n_lat, n_rad, LANES), BF16),
            pltpu.VMEM((own, n_lat * n_rad, LANES), F32),
            pltpu.VMEM((own, PIECES, n_rad, n_lat // PIECES, LANES), BF16),
            pltpu.VMEM((own, PIECES, n_rad, n_lat // PIECES, LANES), BF16),
            pltpu.VMEM((own, n_rad, n_q, full), BF16),
            pltpu.VMEM((own, PIECES, full, c * n_lat), BF16),
            pltpu.VMEM((own, PIECES, n_rad, n_q // PIECES, c * n_lat), BF16),
            dma, dma((n_l,)), dma, dma, dma,
            dma, dma, dma((own,)), dma((own,)),
            dma((own, PIECES)), dma((own, PIECES)), dma((own, PIECES)), dma((own, PIECES)),
        ],
        compiler_params=pltpu.CompilerParams(
            collective_id=0, has_side_effects=True, vmem_limit_bytes=53 << 20
        ),
    )(
        jnp.concatenate([order_of_slot, degree_count, degree_of_slot]).reshape(-1, block),
        rows,
        legendre.reshape(n_deg, n_h),
        inverse,
    )
    return pl.pallas_call(
        widen,
        grid=(own,),
        out_shape=jax.ShapeDtypeStruct((n_rad, own, n_q, c, n_lat), F32),
        in_specs=[
            pl.BlockSpec(
                (1, PIECES, n_rad, n_q // PIECES, c * n_lat), lambda i: (i, 0, 0, 0, 0)
            )
        ],
        out_specs=pl.BlockSpec((n_rad, 1, n_q, c, n_lat), lambda i: (0, i, 0, 0, 0)),
        compiler_params=pltpu.CompilerParams(vmem_limit_bytes=8 << 20),
    )(solved).reshape(n_t, n_q, c, n_lat)


def solution(mesh):
    in_specs = (
        P(None, None, "rad", None, None, "lat"),
        P("lat", None, None),
        P("lat", "rad", None),
        P(),
        P(),
        P(),
    )
    out_specs = P("lat", "rad", None, None)
    body = functools.partial(on_device, mesh.shape["lat"], mesh.shape["rad"])
    return jax.shard_map(
        body, mesh=mesh, in_specs=in_specs, out_specs=out_specs, check_vma=False
    )
```

```python
import functools

import jax
import jax.numpy as jnp
from jax import lax
from jax.experimental import pallas as pl
from jax.experimental.pallas import tpu as pltpu
from jax.sharding import PartitionSpec as P

BF16 = jnp.bfloat16
F32 = jnp.float32
MESH = pl.DeviceIdType.MESH
LANES = 128
PIECES = 2


def iota(shape, dim):
    return lax.broadcasted_iota(jnp.int32, shape, dim)


def column(row):
    return jnp.transpose(jnp.broadcast_to(row, (LANES, row.shape[1])))


def dot_nt(a, b):
    return lax.dot_general(a, b, (((1,), (1,)), ((), ())), preferred_element_type=F32)


def farthest_first(k, n):
    if isinstance(k, int):
        return n // 2 + (-((k + 1) // 2) if k % 2 else k // 2)
    return n // 2 + lax.select(lax.rem(k, 2) == 0, k // 2, -((k + 1) // 2))


def kernel(
    dims,
    small_hbm, rows_hbm, table_hbm, inverse_hbm,
    recv_o,
    small, rows, table, north, south, send_folds, recv_folds,
    natural_degree, pick, column_degree, table_live, send_c, recv_c, wide,
    bring_c, got_c, matrices, right_side, send_o,
    small_sem, rows_sem, table_sem, send0, recv0, send1, recv1, send2, recv2, send3, recv3, send4, recv4,
):
    n_lat, n_rad, n_l, n_deg, n_t = dims
    own = n_t // n_rad
    n_q, full = matrices.shape[2], matrices.shape[3]
    radii = full // 2 // n_rad
    me = lax.axis_index("lat")
    y = lax.axis_index("rad")
    group, planes = 8, n_lat // 8
    z, x, core = me // group, lax.rem(me, group) // 2, lax.rem(me, 2)
    places = [
        lax.rem(x + d, 4) * 2 + lax.rem(core + 1 + i, 2) for d in (2, 1, 3, 0) for i in range(2)
    ]

    def ring_of_planes(k):
        return lax.rem(z + farthest_first(k, planes), planes)

    def rad_peer(k):
        return lax.rem(y + farthest_first(k, n_rad), n_rad)

    load_small = pltpu.make_async_copy(small_hbm, small, small_sem)

    def load_rows(l):
        return pltpu.make_async_copy(rows_hbm.at[:, l], rows.at[l], rows_sem.at[l])

    load_small.start()
    for l in range(n_l):
        load_rows(l).start()
    load_table = pltpu.make_async_copy(table_hbm, table, table_sem)
    load_table.start()

    barrier = pltpu.get_barrier_semaphore()

    def greet_lat(k, carry):
        plane = ring_of_planes(k)
        for place in places:
            pl.semaphore_signal(
                barrier, inc=1, device_id={"lat": plane * group + place}, device_id_type=MESH
            )
        return carry

    def greet_rad(k, carry):
        pl.semaphore_signal(
            barrier, inc=1, device_id={"rad": lax.rem(y + k, n_rad)}, device_id_type=MESH
        )
        return carry

    for k in range(planes - 1):
        greet_lat(k, 0)
    for place in places[:-1]:
        pl.semaphore_signal(
            barrier, inc=1, device_id={"lat": z * group + place}, device_id_type=MESH
        )
    for k in range(1, n_rad):
        greet_rad(k, 0)

    load_small.wait()
    order = small[0:1, :n_lat].astype(F32)
    order_column = column(order)[:, :n_lat]
    order_pick = jnp.where(
        order_column == iota((n_lat, n_lat), 1).astype(F32), 1.0, 0.0
    ).astype(BF16)
    load_rows(0).wait()
    for l in range(1, n_l):
        load_rows(l).wait()
    for l in range(n_l):
        picked = dot_nt(order_pick, rows.at[l].reshape(2 * LANES, n_lat)[...])
        north[pl.ds(l, n_lat, stride=n_l), :] = picked[:, :LANES]
        south[pl.ds(l, n_lat, stride=n_l), :] = picked[:, LANES:]

    source, target = iota((2 * LANES, 2 * LANES), 0), iota((2 * LANES, 2 * LANES), 1)
    fold = jnp.where(
        source // 2 == target % LANES,
        jnp.where((source % 2 == 1) & (target >= LANES), -1.0, 1.0),
        0.0,
    ).astype(BF16)

    def fold_plane(k, carry):
        at = pl.ds(pl.multiple_of(k * (2 * group * n_l), 16), 2 * group * n_l)
        both = jnp.concatenate([north[at, :], south[at, :]], axis=1).astype(BF16)
        folded = jnp.dot(both, fold, preferred_element_type=F32).astype(BF16)
        for p in range(2):
            send_folds.at[p].reshape(n_lat * n_l, LANES)[at, :] = folded[
                :, p * LANES:(p + 1) * LANES
            ]
        return carry

    lax.fori_loop(0, planes // 2, fold_plane, 0)

    pl.semaphore_wait(barrier, n_lat + n_rad - 2)

    def send_folded(peer):
        pltpu.make_async_remote_copy(
            src_ref=send_folds.at[:, peer], dst_ref=recv_folds.at[:, me],
            send_sem=send1, recv_sem=recv1,
            device_id={"lat": peer}, device_id_type=MESH,
        ).start()

    for k in range(planes - 1):
        plane = ring_of_planes(k)
        for place in places:
            send_folded(plane * group + place)
    for place in places[:-1]:
        send_folded(z * group + place)
    pltpu.make_async_copy(send_folds.at[:, me], recv_folds.at[:, me], recv1).start()

    def send_matrices(k, carry):
        peer = rad_peer(k)
        pltpu.make_async_remote_copy(
            src_ref=inverse_hbm.at[pl.ds(peer * own, own)], dst_ref=matrices.at[:, y],
            send_sem=send0, recv_sem=recv0,
            device_id={"rad": peer}, device_id_type=MESH,
        ).start()
        return carry

    lax.fori_loop(0, n_rad - 1, send_matrices, 0)
    pltpu.make_async_copy(inverse_hbm.at[pl.ds(y * own, own)], matrices.at[:, y], recv0).start()

    mine = jnp.sum(jnp.where(iota((1, n_lat), 1) == me, order, 0.0), axis=1, keepdims=True)
    count = jnp.sum(
        jnp.where(iota((1, n_lat), 1).astype(F32) == mine, small[0:1, n_lat:2 * n_lat].astype(F32), 0.0),
        axis=1, keepdims=True,
    )
    first = n_deg - count
    blocks, block = small.shape[0] - 1, small.shape[1]

    def to_column(b, carry):
        at = pl.ds(pl.multiple_of(b * block, block), block)
        natural_degree[at, :] = column(small[pl.ds(b + 1, 1), :].astype(F32))
        return carry

    lax.fori_loop(0, blocks, to_column, 0)
    step = n_deg // own // blocks

    for h in range(own):
        def pick_rows(b, carry):
            held = natural_degree[pl.ds(b * (step * own) + h, step, stride=own), :]
            at = pl.ds(pl.multiple_of(b * step + h * (n_deg // own), step), step)
            column_degree[at, :] = held
            for j in range(blocks):
                lane = (iota((step, block), 1) + j * block).astype(F32)
                cell = held[:, :block]
                pick[at, j * block:(j + 1) * block] = jnp.where(
                    (cell == lane) & (cell >= first), 1.0, 0.0
                ).astype(BF16)
            return carry

        lax.fori_loop(0, blocks, pick_rows, 0)

    load_table.wait()
    rows_at_once = min(256, n_deg // own)

    def order_rows(b, carry):
        at = pl.ds(pl.multiple_of(b * rows_at_once, rows_at_once), rows_at_once)
        table_live[at, :] = jnp.dot(
            pick[at, :], table[...], preferred_element_type=F32
        ).astype(BF16)
        return carry

    lax.fori_loop(0, n_deg // rows_at_once, order_rows, 0)

    pltpu.make_async_copy(recv_folds, recv_folds, recv1).wait()

    parts = n_deg // own // rows_at_once

    reach = planes // parts

    for h in range(own):
        def send(peer):
            pltpu.make_async_remote_copy(
                src_ref=send_c.at[h, peer], dst_ref=recv_c.at[h, me],
                send_sem=send2.at[h], recv_sem=recv2.at[h],
                device_id={"lat": peer}, device_id_type=MESH,
            ).start()

        def analyse_and_send(k, carry):
            part = lax.rem(z // reach + 1 + k, parts)
            begin = pl.multiple_of(part * rows_at_once, rows_at_once)
            at = pl.ds(begin + h * (n_deg // own), rows_at_once)
            both = jnp.concatenate(
                [recv_folds.at[p].reshape(n_lat * n_l, LANES)[...] for p in range(2)], axis=1
            )
            product = jnp.dot(table_live[at, :], both, preferred_element_type=F32)
            parity = (column_degree[at, :] - first).astype(jnp.int32) & 1
            send_c.at[h].reshape(n_lat * n_rad, LANES)[pl.ds(begin, rows_at_once), :] = jnp.where(
                parity == 0, product[:, :LANES], product[:, LANES:]
            ).astype(BF16)

            for j in range(reach):
                plane = part * reach + lax.rem(z + 1 + j, reach)
                for place in places[:-1]:
                    send(plane * group + place)
                last = plane * group + places[-1]
                if j < reach - 1:
                    send(last)
                else:
                    pl.when(last != me)(functools.partial(send, last))
            return carry

        lax.fori_loop(0, parts, analyse_and_send, 0)
        pltpu.make_async_copy(send_c.at[h, me], recv_c.at[h, me], recv2.at[h]).start()

    some = n_lat // PIECES
    for h in range(own):
        pltpu.make_async_copy(recv_c.at[h], recv_c.at[h], recv2.at[h]).wait()
        wide[h] = recv_c.at[h].reshape(n_lat * n_rad, LANES)[...].astype(F32)
        for p in range(PIECES):
            def bring(k, carry):
                peer = rad_peer(k)
                bring_c[h, p, peer] = wide[
                    h, pl.ds(p * some * n_rad + peer, some, stride=n_rad), :
                ].astype(BF16)
                pltpu.make_async_remote_copy(
                    src_ref=bring_c.at[h, p, peer], dst_ref=got_c.at[h, p, y],
                    send_sem=send3.at[h, p], recv_sem=recv3.at[h, p],
                    device_id={"rad": peer}, device_id_type=MESH,
                ).start()
                return carry

            lax.fori_loop(0, n_rad - 1, bring, 0)
            got_c[h, p, y] = wide[
                h, pl.ds(p * some * n_rad + y, some, stride=n_rad), :
            ].astype(BF16)

    pltpu.make_async_copy(matrices, matrices, recv0).wait()
    others = pl.ds(0, n_rad - 1)
    slab = n_q // PIECES
    lanes_of = iota((radii, LANES), 1)
    second_part = lax.rem(lanes_of // some, 2) == 1
    second_half = iota((slab, LANES), 1) >= LANES // PIECES
    for h in range(own):
        for p in range(PIECES):
            pltpu.make_async_copy(
                got_c.at[h, p, others], got_c.at[h, p, others], recv3.at[h, p]
            ).wait()
            for o in range(n_rad):
                block = got_c[h, p, o]
                turned = jnp.transpose(jnp.concatenate([block] * (2 * PIECES), axis=0))
                for f in range(2):
                    at = 2 * f * radii
                    begin = f * (full // 2) + o * radii
                    right_side[h, p, begin:begin + radii, :] = jnp.where(
                        second_part,
                        turned[at + radii:at + 2 * radii, :].astype(F32),
                        turned[at:at + radii, :].astype(F32),
                    ).astype(BF16)
            solved = jnp.dot(
                matrices.at[h].reshape(full, full)[...], right_side[h, p],
                preferred_element_type=F32,
            )
            for o in range(n_rad):
                send_o[h, p, o] = jnp.where(
                    second_half,
                    solved[o * n_q + slab:o * n_q + 2 * slab, :],
                    solved[o * n_q:o * n_q + slab, :],
                ).astype(BF16)

            def give(k, carry):
                peer = rad_peer(k)
                pltpu.make_async_remote_copy(
                    src_ref=send_o.at[h, p, peer], dst_ref=recv_o.at[h, p, y],
                    send_sem=send4.at[h, p], recv_sem=recv4.at[h, p],
                    device_id={"rad": peer}, device_id_type=MESH,
                ).start()
                return carry

            lax.fori_loop(0, n_rad - 1, give, 0)
            pltpu.make_async_copy(
                send_o.at[h, p, y], recv_o.at[h, p, y], recv4.at[h, p]
            ).start()

    for h in range(own):
        for p in range(PIECES):
            pltpu.make_async_copy(recv_o.at[h, p], recv_o.at[h, p], recv4.at[h, p]).wait()

    left = inverse_hbm.at[pl.ds(0, (n_rad - 1) * own)]
    pltpu.make_async_copy(left, left, send0).wait()
    most = pl.ds(0, n_lat - 1)
    pltpu.make_async_copy(send_folds.at[:, most], send_folds.at[:, most], send1).wait()
    for h in range(own):
        pltpu.make_async_copy(send_c.at[h, most], send_c.at[h, most], send2.at[h]).wait()
        for p in range(PIECES):
            sent = bring_c.at[h, p, others]
            pltpu.make_async_copy(sent, sent, send3.at[h, p]).wait()
            sent = send_o.at[h, p, others]
            pltpu.make_async_copy(sent, sent, send4.at[h, p]).wait()


def widen(solved_ref, out_ref):
    n_rad, slab = solved_ref.shape[2:4]
    n_q, n_c, n_lat = out_ref.shape[2:]
    some = n_lat // PIECES
    for o in range(n_rad):
        flat = out_ref.at[o, 0].reshape(n_q * n_c, n_lat)
        block = [solved_ref[0, p, o].astype(F32) for p in range(PIECES)]
        for i in range(PIECES):
            for c in range(n_c):
                begin = (i * n_c + c) * some
                flat[pl.ds(i * slab * n_c + c, slab, stride=n_c), :] = jnp.concatenate(
                    [b[:, begin:begin + some] for b in block], axis=1
                )


def on_device(n_lat, n_rad, fourier, legendre, inverse, order_of_slot, degree_of_slot, degree_count):
    f, c, r, h, m, n_l = fourier.shape
    n_deg, n_h = legendre.shape[1:]
    n_t, n_q, full = inverse.shape
    own = n_t // n_rad
    rows = jnp.transpose(fourier, (0, 1, 2, 5, 3, 4)).reshape(f * c * r, n_l, h, m)
    block = min(LANES, n_deg)
    any_space = pl.BlockSpec(memory_space=pl.ANY)
    dma = pltpu.SemaphoreType.DMA
    pairs = (2, n_lat, n_l // 2, 2, LANES)
    solved = pl.pallas_call(
        functools.partial(kernel, (n_lat, n_rad, n_l, n_deg, n_t)),
        out_shape=jax.ShapeDtypeStruct((own, PIECES, n_rad, n_q // PIECES, c * n_lat), BF16),
        in_specs=[any_space] * 4,
        out_specs=any_space,
        scratch_shapes=[
            pltpu.VMEM((n_deg // block + 1, block), jnp.int32),
            pltpu.VMEM((n_l, f * c * r, h, m), BF16),
            pltpu.VMEM((n_deg, n_h), BF16),
            pltpu.VMEM((n_lat * n_l, LANES), F32),
            pltpu.VMEM((n_lat * n_l, LANES), F32),
            pltpu.VMEM(pairs, BF16),
            pltpu.VMEM(pairs, BF16),
            pltpu.VMEM((n_deg, LANES), F32),
            pltpu.VMEM((n_deg, n_deg), BF16),
            pltpu.VMEM((n_deg, LANES), F32),
            pltpu.VMEM((n_deg, n_h), BF16),
            pltpu.VMEM((own, n_lat, n_rad, LANES), BF16),
            pltpu.VMEM((own, n_lat, n_rad, LANES), BF16),
            pltpu.VMEM((own, n_lat * n_rad, LANES), F32),
            pltpu.VMEM((own, PIECES, n_rad, n_lat // PIECES, LANES), BF16),
            pltpu.VMEM((own, PIECES, n_rad, n_lat // PIECES, LANES), BF16),
            pltpu.VMEM((own, n_rad, n_q, full), BF16),
            pltpu.VMEM((own, PIECES, full, c * n_lat), BF16),
            pltpu.VMEM((own, PIECES, n_rad, n_q // PIECES, c * n_lat), BF16),
            dma, dma((n_l,)), dma, dma, dma,
            dma, dma, dma((own,)), dma((own,)),
            dma((own, PIECES)), dma((own, PIECES)), dma((own, PIECES)), dma((own, PIECES)),
        ],
        compiler_params=pltpu.CompilerParams(
            collective_id=0, has_side_effects=True, vmem_limit_bytes=53 << 20
        ),
    )(
        jnp.concatenate([order_of_slot, degree_count, degree_of_slot]).reshape(-1, block),
        rows,
        legendre.reshape(n_deg, n_h),
        inverse,
    )
    return pl.pallas_call(
        widen,
        grid=(own,),
        out_shape=jax.ShapeDtypeStruct((n_rad, own, n_q, c, n_lat), F32),
        in_specs=[
            pl.BlockSpec(
                (1, PIECES, n_rad, n_q // PIECES, c * n_lat), lambda i: (i, 0, 0, 0, 0)
            )
        ],
        out_specs=pl.BlockSpec((n_rad, 1, n_q, c, n_lat), lambda i: (0, i, 0, 0, 0)),
        compiler_params=pltpu.CompilerParams(vmem_limit_bytes=8 << 20),
    )(solved).reshape(n_t, n_q, c, n_lat)


def solution(mesh):
    in_specs = (
        P(None, None, "rad", None, None, "lat"),
        P("lat", None, None),
        P("lat", "rad", None),
        P(),
        P(),
        P(),
    )
    out_specs = P("lat", "rad", None, None)
    body = functools.partial(on_device, mesh.shape["lat"], mesh.shape["rad"])
    return jax.shard_map(
        body, mesh=mesh, in_specs=in_specs, out_specs=out_specs, check_vma=False
    )
```
